32 devices in a mesh: row: 4 (over y, x), col: 8 (over z, core).
Axes of the slice: x: 2, y: 2, z: 4, core: 2. Of those that a mesh axis runs over, the one named last changes fastest.
Arguments:
- fact_block: int32 [98304, 1], P(('row', 'col')), may hold values from 0 to 31; in each aligned block of 3072 rows (0 to 3071, 3072 to 6143, ...) at most 192 rows name the same one
- fact_offset: int32 [98304], P(('row', 'col')), may hold values from 0 to 2047
- fact_date: int32 [98304], P(('row', 'col')), may hold values from 0 to 2555
- revenue: bfloat16 [98304], P(('row', 'col')), may hold values from 0.5 to 4
- supplier_words: int32 [2208], P('col'), may hold values from 0 to 1073741823
- date_words: int32 [88], P('col'), may hold values from 0 to 1073741823
- candidates: int32 [1024], replicated, may hold values from 0 to 65535
Outputs:
- supplier_revenue: float32 [65536], P(('row', 'col'))
- candidate_revenue: float32 [1024], replicated
- candidate_total: float32 [], replicated
The draws below stay inside these ranges and needn't reach their ends.
Inputs may be any that keep to these rules, and one draw needn't show every extreme that they name: `fact_block`: each device's rows name no owner block more than 192 times. `candidates`: ids may repeat.
All inputs are finite; a program needn't handle non-finite values.
Results may differ from the reference program's by a relative error of at most 0.0003.
Values sent between devices are 32-bit elements; how exact they have to be, the bound alone decides.
A program may use at most 64 MiB of HBM per device.

```python
import math
import jax
import jax.numpy as jnp
import numpy as np

ROWS_DEV = 3072
SUP_DEV = 2048
DATES = 2556
CANDS = 1024
ROWS = 98304
SUPPLIERS = 65536
MASK_WORDS = 69
DATE_WORDS = 88
CAP = 192
DEVICES = 32


def with_ends(entries, stream_key, least, largest):
    spot = [jax.random.randint(jax.random.fold_in(stream_key, axis), (), 0, length) for axis, length in enumerate(entries.shape)]
    main_axis = entries.shape.index(max(entries.shape))
    beside = spot[:main_axis] + [(spot[main_axis] + 1) % entries.shape[main_axis]] + spot[main_axis + 1:]
    return entries.at[tuple(spot)].set(least).at[tuple(beside)].set(largest)


def shard_levels(rng, extent, pieces, least, top_value):
    gain, own = 1.0, jax.random.fold_in(rng, 6)
    for position, parts in pieces:
        draws = jnp.exp(jax.random.uniform(jax.random.fold_in(own, position), (parts,), jnp.float32, least / len(pieces), top_value / len(pieces)))
        gain = gain * jnp.repeat(draws, extent[position] // parts).reshape([-1 if axis == position else 1 for axis in range(len(extent))])
    return gain


def routed_block(stream_key, own, number, rows, amount, top, limit, skew):
    sequence = jax.random.permutation(stream_key, amount)
    heavy_load, usual = load_shares(amount, rows * top, limit, skew, True), load_shares(amount, rows * top, limit, skew, False)
    places = jnp.arange(amount)

    def named(lengths, offset_by):
        used = int((lengths > 0).sum())
        fixed = max(1, used // 4)
        moved = fixed + (places - fixed + offset_by * (used - fixed)) % max(1, amount - fixed)
        return jnp.zeros((amount,), jnp.int32).at[sequence[jnp.where(places < fixed, places, moved)]].set(jnp.asarray(lengths, jnp.int32))

    lengths = jnp.where(number % 4 == 0, named(heavy_load, number // 4), named(usual, number - number // 4 - 1))
    mixed = jax.random.permutation(jax.random.fold_in(own, 3), amount)
    giver, sink = mixed[0:amount // 2 * 2:2], mixed[1:amount // 2 * 2:2]
    margin = jnp.minimum(lengths[giver] - 1, limit - lengths[sink]) // 2
    margin = jnp.where((giver == sequence[0]) | (sink == sequence[0]) | (lengths[sink] == 0), 0, jnp.maximum(margin, 0))
    moved = jax.random.randint(jax.random.fold_in(own, 4), (amount // 2,), 0, 1 << 20) % (margin + 1)
    lengths = lengths.at[giver].add(-moved).at[sink].add(moved)
    items = jnp.searchsorted(jnp.cumsum(lengths), jnp.arange(rows * top), side="right").astype(jnp.int32)
    listing = items.reshape(top, rows).T
    listing = listing[jax.random.permutation(jax.random.fold_in(own, 1), rows)]
    offset_by = jax.random.randint(jax.random.fold_in(own, 2), (rows, 1), 0, top)
    return jnp.take_along_axis(listing, (jnp.arange(top)[None, :] + offset_by) % top, axis=1)


def load_shares(number_of, total, most, skew, full):
    portions = [(1 << 20) // math.isqrt(grade ** skew) + 1 for grade in range(1, number_of + 1)]
    largest = most if full else min(most, max(-(-total // number_of), total * portions[0] // sum(portions)))
    least = 1 if total - largest >= number_of - 1 else 0
    holding, surplus = [largest] + [least] * (number_of - 1), total - largest - least * (number_of - 1)
    while surplus > 0:
        movable = [i for i in range(1, number_of) if holding[i] < largest] or [i for i in range(1, number_of) if holding[i] < most]
        whole, left = sum([portions[i] for i in movable]), surplus
        for i in movable:
            addition = min(most - holding[i], max(1, left * portions[i] // whole), surplus)
            holding[i] = holding[i] + addition
            surplus = surplus - addition
    return np.array(holding)


def setup_inputs(seed: int = 0) -> dict:
    keys = jax.random.split(jax.random.key(seed), 8)
    fact_block_keys = jax.random.split(jax.random.fold_in(keys[0], 1), ROWS // ROWS_DEV)
    fact_block_turns = jax.random.permutation(jax.random.fold_in(keys[0], 3), ROWS // ROWS_DEV)
    fact_block = jax.vmap(lambda own, number: routed_block(jax.random.fold_in(keys[0], 2), own, number, ROWS_DEV, DEVICES, 1, CAP, 1))(fact_block_keys, fact_block_turns).reshape((ROWS, 1))
    fact_offset = with_ends(jax.random.randint(keys[1], (ROWS,), 0, SUP_DEV), jax.random.fold_in(keys[1], 1), 0, SUP_DEV - 1).astype(jnp.int32)
    fact_date = with_ends(jax.random.randint(keys[2], (ROWS,), 0, DATES), jax.random.fold_in(keys[2], 1), 0, DATES - 1).astype(jnp.int32)
    revenue = jnp.clip(jnp.exp(math.log(4.0) - 2.0794415 * jax.random.uniform(keys[3], (ROWS,), jnp.float32) ** shard_levels(keys[3], (ROWS,), ((0, 32),), -0.2, 0.2)), 0.5, 4.0).astype(jnp.bfloat16)
    supplier_words = with_ends(jax.random.randint(keys[4], (DEVICES * MASK_WORDS,), 0, 1073741824), jax.random.fold_in(keys[4], 1), 0, 1073741823).astype(jnp.int32)
    date_words = with_ends(jax.random.randint(keys[5], (DATE_WORDS,), 0, 1073741824), jax.random.fold_in(keys[5], 1), 0, 1073741823).astype(jnp.int32)
    candidates = with_ends(jax.random.randint(keys[6], (CANDS,), 0, SUPPLIERS), jax.random.fold_in(keys[6], 1), 0, SUPPLIERS - 1).astype(jnp.int32)
    return {"fact_block": fact_block, "fact_offset": fact_offset, "fact_date": fact_date, "revenue": revenue, "supplier_words": supplier_words, "date_words": date_words, "candidates": candidates}


def unpack(words, index, place):
    return jnp.bitwise_and(jnp.right_shift(words[index], place), 1)


def reference(fact_block, fact_offset, fact_date, revenue, supplier_words, date_words, candidates):
    owner = fact_block[:, 0]
    supplier_bit = unpack(supplier_words, (owner * MASK_WORDS + fact_offset // 30).astype(jnp.int32), (fact_offset % 30).astype(jnp.int32))
    date_bit = unpack(date_words, (fact_date // 30).astype(jnp.int32), (fact_date % 30).astype(jnp.int32))
    masked = jnp.where(supplier_bit * date_bit == 1, revenue, jnp.zeros_like(revenue))
    global_id = (owner * SUP_DEV + fact_offset).astype(jnp.int32)
    supplier_revenue = jax.ops.segment_sum(masked.astype(jnp.float32), global_id, num_segments=SUPPLIERS)
    candidate_revenue = supplier_revenue[candidates]
    candidate_total = jnp.sum(candidate_revenue)
    return supplier_revenue, candidate_revenue, candidate_total
```

```python
import functools

import jax
import jax.numpy as jnp
from jax import lax
from jax.experimental import pallas as pl
from jax.experimental.pallas import tpu as pltpu
from jax.sharding import PartitionSpec as P

SUP_DEV = 2048
LANES = 128
WIDE = 2 * LANES
GROUP = SUP_DEV // WIDE
BITS = 30
CORES = 2
SLAB = 4
MESH = pl.DeviceIdType.MESH


def div_bits(x):
    return lax.shift_right_logical(x * 2185, 16)


def lookup(row, index):
    table = jnp.broadcast_to(row, index.shape)
    return jnp.take_along_axis(table, index, axis=1, mode="promise_in_bounds")


def kernel(
    rows_axis, cols_axis,
    block_in, offset_in, date_in, rev_in, cand_in, sup_in, dat_in,
    both_ref,
    block_ref, offset_ref, date_ref, rev_ref, cand_ref, load_sem,
    pack, hot, hist, dat_buf, sup_buf, part, cpart, cparts,
    ready, ready_plane, dat_send, dat_recv, sup_send, sup_recv, row_send, row_recv,
    h_send, h_recv, c_send, c_recv,
):
    R, C = rows_axis, cols_axis
    Z, Q = C // CORES, R * CORES
    i, j = lax.axis_index("row"), lax.axis_index("col")
    z, core = j // CORES, j % CORES
    q = i * CORES + core
    n_rows = block_ref.shape[0]
    n_words = sup_in.shape[0]
    per_block = n_words // R
    owned_rows = both_ref.shape[0] - cand_ref.shape[0]
    lines = R * C * GROUP
    tall = min(lines, WIDE)

    pairs = [
        (offset_in, offset_ref), (block_in, block_ref), (date_in, date_ref), (rev_in, rev_ref),
        (cand_in, cand_ref), (dat_in, dat_buf.at[j]), (sup_in, sup_buf.at[j, 0]),
    ]
    loads = [pltpu.make_async_copy(src, dst, load_sem.at[n]) for n, (src, dst) in enumerate(pairs)]
    for load in loads:
        load.start()

    barrier = pltpu.get_barrier_semaphore()

    def loop(low, high, body):
        def step(n, carry):
            body(n)
            return carry

        lax.fori_loop(low, high, step, 0)

    def at_plane(p):
        return (p // CORES, z * CORES + p % CORES)

    def greet(peer):
        pl.semaphore_signal(barrier, inc=1, device_id=peer, device_id_type=MESH)

    loop(j + 1, C, lambda p: greet((i, p)))
    loop(CORES * (i + 1), Q, lambda p: greet(at_plane(p)))

    @pl.when(j + CORES * i > 0)
    def _():
        pl.semaphore_wait(barrier, j + CORES * i)

    def answer(p):
        pl.semaphore_signal(ready.at[j], inc=1, device_id=(i, p), device_id_type=MESH)

    def answer_plane(p):
        pl.semaphore_signal(ready_plane, inc=1, device_id=at_plane(p), device_id_type=MESH)

    def remote(src, dst, send, recv, peer):
        return pltpu.make_async_remote_copy(
            src_ref=src, dst_ref=dst, send_sem=send, recv_sem=recv, device_id=peer, device_id_type=MESH
        )

    def dat_copy(p, source):
        return remote(dat_in, dat_buf.at[source], dat_send.at[p], dat_recv.at[source], (i, p))

    def sup_copy(p, source):
        return remote(sup_in, sup_buf.at[source, 0], sup_send.at[p], sup_recv.at[source], (i, p))

    def row_copy(p, source):
        return remote(pack.at[z], pack.at[source], row_send.at[p], row_recv.at[source], (i, p * CORES + core))

    loop(0, j, lambda p: dat_copy(p, j).start())
    loop(0, j, answer)
    loop(0, CORES * i, answer_plane)

    for load in loads[:4]:
        load.wait()
    pack[z, :n_rows] = (block_ref[...] * SUP_DEV + offset_ref[...]).astype(jnp.float32)
    pack[z, n_rows : 2 * n_rows] = date_ref[...].astype(jnp.float32)
    pack[z, 2 * n_rows :] = rev_ref[...].astype(jnp.float32)
    loop(0, z, lambda p: row_copy(p, z).start())

    for load in loads[4:]:
        load.wait()

    def to_later(p):
        pl.semaphore_wait(ready.at[p], 1)
        dat_copy(p, j).start()

        @pl.when(p % CORES == core)
        def _():
            row_copy(p // CORES, z).start()

    loop(0, j, lambda p: sup_copy(p, j).start())

    cand = cand_ref[...]
    groups = cand.shape[0]
    c_owner = lax.shift_right_logical(cand, 11)
    c_off = cand & (SUP_DEV - 1)
    c_line = c_owner * GROUP + (lax.shift_right_logical(c_off, 7) & (GROUP - 1))
    c_col = lax.shift_right_logical(c_off, 10) * LANES + (c_off & (LANES - 1))
    iota = lax.broadcasted_iota(jnp.int32, (WIDE, LANES), 0)
    for g in range(groups):
        hit = iota == c_col[g : g + 1, :]
        hot[:, g * LANES : (g + 1) * LANES] = jnp.where(hit, 1.0, 0.0).astype(jnp.bfloat16)

    loop(j + 1, C, to_later)
    loop(j + 1, C, lambda p: sup_copy(p, j).start())

    def others(n, me, body):
        loop(0, me, body)
        loop(me + 1, n, body)

    others(C, j, lambda p: dat_copy(p, p).wait_recv())
    table = jnp.concatenate(
        [dat_buf[c] for c in range(C)] + [jnp.zeros((1, LANES - C * dat_in.shape[1]), jnp.int32)], axis=1
    )

    short = iota.astype(jnp.int16)
    one, nought = jnp.ones((), jnp.bfloat16), jnp.zeros((), jnp.bfloat16)

    def spread(x, r):
        return jnp.broadcast_to(x[r : r + 1, :], (WIDE, LANES))

    def add_rows(source, base, total):
        ids = pack[source, :n_rows].astype(jnp.int32)
        day = pack[source, n_rows : 2 * n_rows].astype(jnp.int32)
        day_word = div_bits(day)
        lit = lax.shift_right_logical(lookup(table, day_word), day - day_word * BITS) & 1
        value = jnp.where(lit == 1, pack[source, 2 * n_rows :], 0.0)
        line = lax.shift_right_logical(ids, 11) * GROUP + (lax.shift_right_logical(ids, 7) & (GROUP - 1)) - base
        column = (lax.shift_right_logical(ids, 10) & 1) * LANES + (ids & (LANES - 1))
        for r in range(0, n_rows, SLAB):
            left = [
                jnp.where(
                    short == spread(line, n).astype(jnp.int16), spread(value, n).astype(jnp.bfloat16), nought
                )[:tall]
                for n in range(r, min(r + SLAB, n_rows))
            ]
            right = [
                jnp.where(short == spread(column, n).astype(jnp.int16), one, nought)
                for n in range(r, min(r + SLAB, n_rows))
            ]
            total = total + lax.dot_general(
                jnp.concatenate(left, axis=1), jnp.concatenate(right, axis=1), (((1,), (1,)), ((), ())),
                preferred_element_type=jnp.float32,
            )
        return total

    def candidates_of(total, base):
        first = total.astype(jnp.bfloat16)
        second = (total - first.astype(jnp.float32)).astype(jnp.bfloat16)
        found = jnp.dot(first, hot[...], preferred_element_type=jnp.float32)
        found = found + jnp.dot(second, hot[...], preferred_element_type=jnp.float32)
        picked = []
        for g in range(groups):
            hit = iota[:tall] == c_line[g : g + 1, :] - base
            picked.append(jnp.sum(jnp.where(hit, found[:, g * LANES : (g + 1) * LANES], 0.0), axis=0, keepdims=True))
        return jnp.concatenate(picked, axis=0)

    empty = jnp.zeros((tall, WIDE), jnp.float32)
    if lines == tall:
        total = add_rows(z, 0, empty)
        for k in range(1, Z):
            source = lax.rem(z + k, Z)
            row_copy(source, source).wait_recv()
            total = add_rows(source, 0, total)
        hist[...] = total
    else:
        others(Z, z, lambda p: row_copy(p, p).wait_recv())

        def fill(t, carry):
            base = pl.multiple_of(t * tall, tall)
            hist[pl.ds(base, tall), :] = lax.fori_loop(0, Z, lambda s, acc: add_rows(s, base, acc), empty)
            return carry

        lax.fori_loop(0, lines // tall, fill, 0)

    plane = [lax.rem(q + k, Q) for k in range(1, Q)]

    @pl.when(i < R - 1)
    def _():
        pl.semaphore_wait(ready_plane, CORES * (R - 1 - i))

    def lines_of(p):
        owner = (p // CORES) * C + z * CORES + p % CORES
        return hist.at[pl.ds(pl.multiple_of(owner * GROUP, GROUP), GROUP), :]

    h_copies = [
        remote(lines_of(p), part.at[k], h_send.at[k], h_recv.at[k], at_plane(p)) for k, p in enumerate(plane)
    ]
    for copy in h_copies:
        copy.start()

    if lines == tall:
        mine = candidates_of(hist[...], 0)
    else:

        def gather(t, acc):
            base = pl.multiple_of(t * tall, tall)
            return acc + candidates_of(hist[pl.ds(base, tall), :], base)

        mine = lax.fori_loop(0, lines // tall, gather, jnp.zeros(cand.shape, jnp.float32))
    cpart[...] = mine
    c_copies = [
        remote(cpart, cparts.at[k], c_send.at[k], c_recv.at[k], at_plane(p)) for k, p in enumerate(plane)
    ]
    for copy in c_copies:
        copy.start()

    others(C, j, lambda p: sup_copy(p, p).wait_recv())
    full = n_words // LANES

    def words_at(source, flat):
        word = lookup(sup_buf[source, :, n_words - LANES :], jnp.maximum(flat - (n_words - LANES), 0))
        for t in range(full):
            near = (flat >= t * LANES) & (flat < (t + 1) * LANES)
            word = jnp.where(near, lookup(sup_buf[source, :, t * LANES : (t + 1) * LANES], flat & (LANES - 1)), word)
        return word

    c_word = div_bits(c_off)
    c_bit = c_off - c_word * BITS
    c_source = lax.div(c_owner, R)
    c_flat = (c_owner - c_source * R) * per_block + c_word

    def word_of(source, acc):
        return jnp.where(c_source == source, words_at(source, c_flat), acc)

    c_words = lax.fori_loop(0, C, word_of, jnp.zeros(cand.shape, jnp.int32))
    c_lit = (lax.shift_right_logical(c_words, c_bit) & 1) == 1

    me = i * C + j
    shape = (owned_rows, LANES)
    spot = lax.broadcasted_iota(jnp.int32, shape, 0) * LANES + lax.broadcasted_iota(jnp.int32, shape, 1)
    spot_word = div_bits(spot)
    my_words = words_at(me // R, lax.rem(me, R) * per_block + spot_word)
    my_lit = (lax.shift_right_logical(my_words, spot - spot_word * BITS) & 1) == 1

    owned = hist[pl.ds(pl.multiple_of(me * GROUP, GROUP), GROUP), :]
    for k, copy in enumerate(h_copies):
        copy.wait_recv()
        owned = owned + part[k]
    both_ref[:GROUP, :] = jnp.where(my_lit[:GROUP], owned[:, :LANES], 0.0)
    both_ref[GROUP:owned_rows, :] = jnp.where(my_lit[GROUP:], owned[:, LANES:], 0.0)

    found = cpart[...]
    for k, copy in enumerate(c_copies):
        copy.wait_recv()
        found = found + cparts[k]
    both_ref[owned_rows:, :] = jnp.where(c_lit, found, 0.0)

    others(C, j, lambda p: dat_copy(p, j).wait_send())
    others(C, j, lambda p: sup_copy(p, j).wait_send())
    others(Z, z, lambda p: row_copy(p, z).wait_send())
    for copy in h_copies + c_copies:
        copy.wait_send()


def finish(both_ref, owned_ref, cand_out_ref, total_ref):
    owned_rows = owned_ref.shape[0]
    owned_ref[...] = both_ref[:owned_rows, :]
    found = both_ref[owned_rows:, :]
    cand_out_ref[...] = found
    total_ref[0, 0] = jnp.sum(found)


def per_device(R, C, fact_block, fact_offset, fact_date, revenue, supplier_words, date_words, candidates):
    rows = fact_offset.shape[0] // LANES
    cands = candidates.shape[0] // LANES
    Z, Q = C // CORES, R * CORES
    f32, i32 = jnp.float32, jnp.int32
    dma = pltpu.SemaphoreType.DMA
    vmem = pl.BlockSpec(memory_space=pltpu.VMEM)
    both = pl.pallas_call(
        functools.partial(kernel, R, C),
        out_shape=jax.ShapeDtypeStruct((SUP_DEV // LANES + cands, LANES), f32),
        in_specs=[pl.BlockSpec(memory_space=pl.ANY)] * 7,
        out_specs=vmem,
        scratch_shapes=[
            pltpu.VMEM((rows, LANES), i32),
            pltpu.VMEM((rows, LANES), i32),
            pltpu.VMEM((rows, LANES), i32),
            pltpu.VMEM((rows, LANES), revenue.dtype),
            pltpu.VMEM((cands, LANES), i32),
            dma((7,)),
            pltpu.VMEM((Z, 3 * rows, LANES), f32),
            pltpu.VMEM((WIDE, cands * LANES), jnp.bfloat16),
            pltpu.VMEM((R * C * GROUP, WIDE), f32),
            pltpu.VMEM((C, 1, date_words.shape[0]), i32),
            pltpu.VMEM((C, 1, supplier_words.shape[0]), i32),
            pltpu.VMEM((Q - 1, GROUP, WIDE), f32),
            pltpu.VMEM((cands, LANES), f32),
            pltpu.VMEM((Q - 1, cands, LANES), f32),
            pltpu.SemaphoreType.REGULAR((C,)),
            pltpu.SemaphoreType.REGULAR,
            dma((C,)), dma((C,)), dma((C,)), dma((C,)), dma((Z,)), dma((Z,)),
            dma((Q - 1,)), dma((Q - 1,)), dma((Q - 1,)), dma((Q - 1,)),
        ],
        compiler_params=pltpu.CompilerParams(collective_id=0, has_side_effects=True),
        name="revenue",
    )(
        fact_block.reshape(rows, LANES),
        fact_offset.reshape(rows, LANES),
        fact_date.reshape(rows, LANES),
        revenue.reshape(rows, LANES),
        candidates.reshape(cands, LANES),
        supplier_words,
        date_words.reshape(1, -1),
    )
    owned, found, total = pl.pallas_call(
        finish,
        out_shape=(
            jax.ShapeDtypeStruct((SUP_DEV // LANES, LANES), f32),
            jax.ShapeDtypeStruct((cands, LANES), f32),
            jax.ShapeDtypeStruct((1, 1), f32),
        ),
        in_specs=[vmem],
        out_specs=(vmem, vmem, pl.BlockSpec(memory_space=pltpu.SMEM)),
        name="finish",
    )(both)
    return owned.reshape(SUP_DEV), found.reshape(candidates.shape), total.reshape(())


def solution(mesh):
    in_specs = (
        P(("row", "col"), None),
        P(("row", "col")),
        P(("row", "col")),
        P(("row", "col")),
        P("col"),
        P("col"),
        P(),
    )
    out_specs = (P(("row", "col")), P(), P())
    body = functools.partial(per_device, mesh.shape["row"], mesh.shape["col"])
    return jax.shard_map(body, mesh=mesh, in_specs=in_specs, out_specs=out_specs, check_vma=False)
```

```python
import functools

import jax
import jax.numpy as jnp
from jax import lax
from jax.experimental import pallas as pl
from jax.experimental.pallas import tpu as pltpu
from jax.sharding import PartitionSpec as P

SUP_DEV = 2048
LANES = 128
WIDE = 2 * LANES
GROUP = SUP_DEV // WIDE
BITS = 30
CORES = 2
SLAB = 4
KERNEL_VMEM = 40 << 20
FINISH_VMEM = 1 << 20
MESH = pl.DeviceIdType.MESH


def div_bits(x):
    return lax.shift_right_logical(x * 2185, 16)


def lookup(row, index):
    table = jnp.broadcast_to(row, index.shape)
    return jnp.take_along_axis(table, index, axis=1, mode="promise_in_bounds")


def kernel(
    rows_axis, cols_axis,
    block_in, offset_in, date_in, rev_in, cand_in, sup_in, dat_in,
    both_ref,
    block_ref, offset_ref, date_ref, rev_ref, cand_ref, load_sem,
    pack, hot, hist, dat_buf, sup_buf, part, cpart, cparts,
    ready, ready_plane, dat_send, dat_recv, sup_send, sup_recv, row_send, row_recv,
    h_send, h_recv, c_send, c_recv,
):
    R, C = rows_axis, cols_axis
    Z, Q = C // CORES, R * CORES
    i, j = lax.axis_index("row"), lax.axis_index("col")
    z, core = j // CORES, j % CORES
    q = i * CORES + core
    n_rows = block_ref.shape[0]
    n_words = sup_in.shape[0]
    per_block = n_words // R
    owned_rows = both_ref.shape[0] - cand_ref.shape[0]
    lines = R * C * GROUP
    tall = min(lines, WIDE)

    pairs = [
        (offset_in, offset_ref), (block_in, block_ref), (date_in, date_ref), (rev_in, rev_ref),
        (cand_in, cand_ref), (dat_in, dat_buf.at[j]), (sup_in, sup_buf.at[j, 0]),
    ]
    loads = [pltpu.make_async_copy(src, dst, load_sem.at[n]) for n, (src, dst) in enumerate(pairs)]
    for load in loads:
        load.start()

    barrier = pltpu.get_barrier_semaphore()

    def loop(low, high, body):
        def step(n, carry):
            body(n)
            return carry

        lax.fori_loop(low, high, step, 0)

    def at_plane(p):
        return (p // CORES, z * CORES + p % CORES)

    def greet(peer):
        pl.semaphore_signal(barrier, inc=1, device_id=peer, device_id_type=MESH)

    loop(j + 1, C, lambda p: greet((i, p)))
    loop(CORES * (i + 1), Q, lambda p: greet(at_plane(p)))

    @pl.when(j + CORES * i > 0)
    def _():
        pl.semaphore_wait(barrier, j + CORES * i)

    def answer(p):
        pl.semaphore_signal(ready.at[j], inc=1, device_id=(i, p), device_id_type=MESH)

    def answer_plane(p):
        pl.semaphore_signal(ready_plane, inc=1, device_id=at_plane(p), device_id_type=MESH)

    def remote(src, dst, send, recv, peer):
        return pltpu.make_async_remote_copy(
            src_ref=src, dst_ref=dst, send_sem=send, recv_sem=recv, device_id=peer, device_id_type=MESH
        )

    def dat_copy(p, source):
        return remote(dat_in, dat_buf.at[source], dat_send.at[p], dat_recv.at[source], (i, p))

    def sup_copy(p, source):
        return remote(sup_in, sup_buf.at[source, 0], sup_send.at[p], sup_recv.at[source], (i, p))

    def row_copy(p, source):
        return remote(pack.at[z], pack.at[source], row_send.at[p], row_recv.at[source], (i, p * CORES + core))

    loop(0, j, lambda p: dat_copy(p, j).start())
    loop(0, j, answer)
    loop(0, CORES * i, answer_plane)

    for load in loads[:4]:
        load.wait()
    pack[z, :n_rows] = (block_ref[...] * SUP_DEV + offset_ref[...]).astype(jnp.float32)
    pack[z, n_rows : 2 * n_rows] = date_ref[...].astype(jnp.float32)
    pack[z, 2 * n_rows :] = rev_ref[...].astype(jnp.float32)
    loop(0, jnp.minimum(z, 1), lambda p: row_copy(p, z).start())

    for load in loads[4:]:
        load.wait()

    def to_later(p):
        pl.semaphore_wait(ready.at[p], 1)
        dat_copy(p, j).start()

        @pl.when(p % CORES == core)
        def _():
            row_copy(p // CORES, z).start()

    loop(0, j, lambda p: sup_copy(p, j).start())

    cand = cand_ref[...]
    groups = cand.shape[0]
    c_owner = lax.shift_right_logical(cand, 11)
    c_off = cand & (SUP_DEV - 1)
    c_line = c_owner * GROUP + (lax.shift_right_logical(c_off, 7) & (GROUP - 1))
    c_col = lax.shift_right_logical(c_off, 10) * LANES + (c_off & (LANES - 1))
    iota = lax.broadcasted_iota(jnp.int32, (WIDE, LANES), 0)
    for g in range(groups):
        hit = iota == c_col[g : g + 1, :]
        hot[:, g * LANES : (g + 1) * LANES] = jnp.where(hit, 1.0, 0.0).astype(jnp.bfloat16)

    loop(j + 1, C, to_later)
    loop(1, z, lambda p: row_copy(p, z).start())
    loop(j + 1, C, lambda p: sup_copy(p, j).start())

    def others(n, me, body):
        loop(0, me, body)
        loop(me + 1, n, body)

    others(C, j, lambda p: dat_copy(p, p).wait_recv())
    table = jnp.concatenate(
        [dat_buf[c] for c in range(C)] + [jnp.zeros((1, LANES - C * dat_in.shape[1]), jnp.int32)], axis=1
    )

    short = iota.astype(jnp.int16)
    one, nought = jnp.ones((), jnp.bfloat16), jnp.zeros((), jnp.bfloat16)

    def spread(x, r):
        return jnp.broadcast_to(x[r : r + 1, :], (WIDE, LANES))

    def add_rows(source, base, total):
        ids = pack[source, :n_rows].astype(jnp.int32)
        day = pack[source, n_rows : 2 * n_rows].astype(jnp.int32)
        day_word = div_bits(day)
        lit = lax.shift_right_logical(lookup(table, day_word), day - day_word * BITS) & 1
        value = jnp.where(lit == 1, pack[source, 2 * n_rows :], 0.0)
        line = lax.shift_right_logical(ids, 11) * GROUP + (lax.shift_right_logical(ids, 7) & (GROUP - 1)) - base
        column = (lax.shift_right_logical(ids, 10) & 1) * LANES + (ids & (LANES - 1))
        for r in range(0, n_rows, SLAB):
            left = [
                jnp.where(
                    short == spread(line, n).astype(jnp.int16), spread(value, n).astype(jnp.bfloat16), nought
                )[:tall]
                for n in range(r, min(r + SLAB, n_rows))
            ]
            right = [
                jnp.where(short == spread(column, n).astype(jnp.int16), one, nought)
                for n in range(r, min(r + SLAB, n_rows))
            ]
            total = total + lax.dot_general(
                jnp.concatenate(left, axis=1), jnp.concatenate(right, axis=1), (((1,), (1,)), ((), ())),
                preferred_element_type=jnp.float32,
            )
        return total

    def candidates_of(total, base):
        first = total.astype(jnp.bfloat16)
        second = (total - first.astype(jnp.float32)).astype(jnp.bfloat16)
        found = jnp.dot(first, hot[...], preferred_element_type=jnp.float32)
        found = found + jnp.dot(second, hot[...], preferred_element_type=jnp.float32)
        picked = []
        for g in range(groups):
            hit = iota[:tall] == c_line[g : g + 1, :] - base
            picked.append(jnp.sum(jnp.where(hit, found[:, g * LANES : (g + 1) * LANES], 0.0), axis=0, keepdims=True))
        return jnp.concatenate(picked, axis=0)

    empty = jnp.zeros((tall, WIDE), jnp.float32)
    if lines == tall:
        sources = [lax.rem(z + k, Z) for k in range(Z)]
        total = empty
        for batch in (sources[:-1], sources[-1:]):
            for source in batch:
                if source is not sources[0]:
                    row_copy(source, source).wait_recv()
            for source in batch:
                total = add_rows(source, 0, total)
        hist[...] = total
    else:
        others(Z, z, lambda p: row_copy(p, p).wait_recv())

        def fill(t, carry):
            base = pl.multiple_of(t * tall, tall)
            hist[pl.ds(base, tall), :] = lax.fori_loop(0, Z, lambda s, acc: add_rows(s, base, acc), empty)
            return carry

        lax.fori_loop(0, lines // tall, fill, 0)

    plane = [lax.rem(q + k, Q) for k in range(1, Q)]

    @pl.when(i < R - 1)
    def _():
        pl.semaphore_wait(ready_plane, CORES * (R - 1 - i))

    def lines_of(p):
        owner = (p // CORES) * C + z * CORES + p % CORES
        return hist.at[pl.ds(pl.multiple_of(owner * GROUP, GROUP), GROUP), :]

    h_copies = [
        remote(lines_of(p), part.at[k], h_send.at[k], h_recv.at[k], at_plane(p)) for k, p in enumerate(plane)
    ]
    for copy in h_copies:
        copy.start()

    if lines == tall:
        mine = candidates_of(hist[...], 0)
    else:

        def gather(t, acc):
            base = pl.multiple_of(t * tall, tall)
            return acc + candidates_of(hist[pl.ds(base, tall), :], base)

        mine = lax.fori_loop(0, lines // tall, gather, jnp.zeros(cand.shape, jnp.float32))
    cpart[...] = mine
    c_copies = [
        remote(cpart, cparts.at[k], c_send.at[k], c_recv.at[k], at_plane(p)) for k, p in enumerate(plane)
    ]
    for copy in c_copies:
        copy.start()

    others(C, j, lambda p: sup_copy(p, p).wait_recv())
    full = n_words // LANES

    def words_at(source, flat):
        word = lookup(sup_buf[source, :, n_words - LANES :], jnp.maximum(flat - (n_words - LANES), 0))
        for t in range(full):
            near = (flat >= t * LANES) & (flat < (t + 1) * LANES)
            word = jnp.where(near, lookup(sup_buf[source, :, t * LANES : (t + 1) * LANES], flat & (LANES - 1)), word)
        return word

    c_word = div_bits(c_off)
    c_bit = c_off - c_word * BITS
    c_source = lax.div(c_owner, R)
    c_flat = (c_owner - c_source * R) * per_block + c_word

    def word_of(source, acc):
        return jnp.where(c_source == source, words_at(source, c_flat), acc)

    c_words = lax.fori_loop(0, C, word_of, jnp.zeros(cand.shape, jnp.int32))
    c_lit = (lax.shift_right_logical(c_words, c_bit) & 1) == 1

    me = i * C + j
    shape = (owned_rows, LANES)
    spot = lax.broadcasted_iota(jnp.int32, shape, 0) * LANES + lax.broadcasted_iota(jnp.int32, shape, 1)
    spot_word = div_bits(spot)
    my_words = words_at(me // R, lax.rem(me, R) * per_block + spot_word)
    my_lit = (lax.shift_right_logical(my_words, spot - spot_word * BITS) & 1) == 1

    owned = hist[pl.ds(pl.multiple_of(me * GROUP, GROUP), GROUP), :]
    for k, copy in enumerate(h_copies):
        copy.wait_recv()
        owned = owned + part[k]
    both_ref[:GROUP, :] = jnp.where(my_lit[:GROUP], owned[:, :LANES], 0.0)
    both_ref[GROUP:owned_rows, :] = jnp.where(my_lit[GROUP:], owned[:, LANES:], 0.0)

    found = cpart[...]
    for k, copy in enumerate(c_copies):
        copy.wait_recv()
        found = found + cparts[k]
    both_ref[owned_rows:, :] = jnp.where(c_lit, found, 0.0)

    others(C, j, lambda p: dat_copy(p, j).wait_send())
    others(C, j, lambda p: sup_copy(p, j).wait_send())
    others(Z, z, lambda p: row_copy(p, z).wait_send())
    for copy in h_copies + c_copies:
        copy.wait_send()


def in_hbm(x):
    return pltpu.with_memory_space_constraint(x, pltpu.HBM)


def finish(both_ref, owned_ref, cand_out_ref, total_ref):
    owned_rows = owned_ref.shape[0]
    owned_ref[...] = both_ref[:owned_rows, :]
    found = both_ref[owned_rows:, :]
    cand_out_ref[...] = found
    total_ref[0, 0] = jnp.sum(found)


def per_device(R, C, fact_block, fact_offset, fact_date, revenue, supplier_words, date_words, candidates):
    rows = fact_offset.shape[0] // LANES
    cands = candidates.shape[0] // LANES
    Z, Q = C // CORES, R * CORES
    f32, i32 = jnp.float32, jnp.int32
    dma = pltpu.SemaphoreType.DMA
    vmem = pl.BlockSpec(memory_space=pltpu.VMEM)
    both = pl.pallas_call(
        functools.partial(kernel, R, C),
        out_shape=jax.ShapeDtypeStruct((SUP_DEV // LANES + cands, LANES), f32),
        in_specs=[pl.BlockSpec(memory_space=pl.ANY)] * 7,
        out_specs=vmem,
        scratch_shapes=[
            pltpu.VMEM((rows, LANES), i32),
            pltpu.VMEM((rows, LANES), i32),
            pltpu.VMEM((rows, LANES), i32),
            pltpu.VMEM((rows, LANES), revenue.dtype),
            pltpu.VMEM((cands, LANES), i32),
            dma((7,)),
            pltpu.VMEM((Z, 3 * rows, LANES), f32),
            pltpu.VMEM((WIDE, cands * LANES), jnp.bfloat16),
            pltpu.VMEM((R * C * GROUP, WIDE), f32),
            pltpu.VMEM((C, 1, date_words.shape[0]), i32),
            pltpu.VMEM((C, 1, supplier_words.shape[0]), i32),
            pltpu.VMEM((Q - 1, GROUP, WIDE), f32),
            pltpu.VMEM((cands, LANES), f32),
            pltpu.VMEM((Q - 1, cands, LANES), f32),
            pltpu.SemaphoreType.REGULAR((C,)),
            pltpu.SemaphoreType.REGULAR,
            dma((C,)), dma((C,)), dma((C,)), dma((C,)), dma((Z,)), dma((Z,)),
            dma((Q - 1,)), dma((Q - 1,)), dma((Q - 1,)), dma((Q - 1,)),
        ],
        compiler_params=pltpu.CompilerParams(
            collective_id=0, has_side_effects=True, vmem_limit_bytes=KERNEL_VMEM
        ),
        name="revenue",
    )(
        in_hbm(fact_block.reshape(rows, LANES)),
        in_hbm(fact_offset.reshape(rows, LANES)),
        in_hbm(fact_date.reshape(rows, LANES)),
        in_hbm(revenue.reshape(rows, LANES)),
        in_hbm(candidates.reshape(cands, LANES)),
        in_hbm(supplier_words),
        in_hbm(date_words.reshape(1, -1)),
    )
    owned, found, total = pl.pallas_call(
        finish,
        out_shape=(
            jax.ShapeDtypeStruct((SUP_DEV // LANES, LANES), f32),
            jax.ShapeDtypeStruct((cands, LANES), f32),
            jax.ShapeDtypeStruct((1, 1), f32),
        ),
        in_specs=[vmem],
        out_specs=(vmem, vmem, pl.BlockSpec(memory_space=pltpu.SMEM)),
        compiler_params=pltpu.CompilerParams(vmem_limit_bytes=FINISH_VMEM),
        name="finish",
    )(both)
    return owned.reshape(SUP_DEV), found.reshape(candidates.shape), total.reshape(())


def solution(mesh):
    in_specs = (
        P(("row", "col"), None),
        P(("row", "col")),
        P(("row", "col")),
        P(("row", "col")),
        P("col"),
        P("col"),
        P(),
    )
    out_specs = (P(("row", "col")), P(), P())
    body = functools.partial(per_device, mesh.shape["row"], mesh.shape["col"])
    return jax.shard_map(body, mesh=mesh, in_specs=in_specs, out_specs=out_specs, check_vma=False)
```

```python
import functools

import jax
import jax.numpy as jnp
from jax import lax
from jax.experimental import pallas as pl
from jax.experimental.pallas import tpu as pltpu
from jax.sharding import PartitionSpec as P

SUP_DEV = 2048
LANES = 128
WIDE = 2 * LANES
GROUP = SUP_DEV // WIDE
BITS = 30
CORES = 2
SLAB = 4
KERNEL_VMEM = 40 << 20
FINISH_VMEM = 1 << 20
MESH = pl.DeviceIdType.MESH


def div_bits(x):
    return lax.shift_right_logical(x * 2185, 16)


def lookup(row, index):
    table = jnp.broadcast_to(row, index.shape)
    return jnp.take_along_axis(table, index, axis=1, mode="promise_in_bounds")


def kernel(
    rows_axis, cols_axis,
    block_in, offset_in, date_in, rev_in, cand_in, sup_in, dat_in,
    both_ref,
    block_ref, offset_ref, date_ref, rev_ref, cand_ref, load_sem,
    pack, hot, hist, dat_buf, sup_buf, part, cpart, cparts,
    ready, ready_plane, dat_send, dat_recv, sup_send, sup_recv, row_send, row_recv,
    h_send, h_recv, c_send, c_recv,
):
    R, C = rows_axis, cols_axis
    Z, Q = C // CORES, R * CORES
    i, j = lax.axis_index("row"), lax.axis_index("col")
    z, core = j // CORES, j % CORES
    q = i * CORES + core
    n_rows = block_ref.shape[0]
    n_words = sup_in.shape[0]
    per_block = n_words // R
    owned_rows = both_ref.shape[0] - cand_ref.shape[0]
    lines = R * C * GROUP
    tall = min(lines, WIDE)

    pairs = [
        (offset_in, offset_ref), (block_in, block_ref), (date_in, date_ref), (rev_in, rev_ref),
        (cand_in, cand_ref), (dat_in, dat_buf.at[j]), (sup_in, sup_buf.at[j, 0]),
    ]
    loads = [pltpu.make_async_copy(src, dst, load_sem.at[n]) for n, (src, dst) in enumerate(pairs)]
    for load in loads:
        load.start()

    barrier = pltpu.get_barrier_semaphore()

    def loop(low, high, body):
        def step(n, carry):
            body(n)
            return carry

        lax.fori_loop(low, high, step, 0)

    def at_plane(p):
        return (p // CORES, z * CORES + p % CORES)

    def greet(peer):
        pl.semaphore_signal(barrier, inc=1, device_id=peer, device_id_type=MESH)

    loop(j + 1, C, lambda p: greet((i, p)))
    loop(CORES * (i + 1), Q, lambda p: greet(at_plane(p)))

    @pl.when(j + CORES * i > 0)
    def _():
        pl.semaphore_wait(barrier, j + CORES * i)

    def answer(p):
        pl.semaphore_signal(ready.at[j], inc=1, device_id=(i, p), device_id_type=MESH)

    def answer_plane(p):
        pl.semaphore_signal(ready_plane, inc=1, device_id=at_plane(p), device_id_type=MESH)

    def remote(src, dst, send, recv, peer):
        return pltpu.make_async_remote_copy(
            src_ref=src, dst_ref=dst, send_sem=send, recv_sem=recv, device_id=peer, device_id_type=MESH
        )

    def dat_copy(p, source):
        return remote(dat_in, dat_buf.at[source], dat_send.at[p], dat_recv.at[source], (i, p))

    def sup_copy(p, source):
        return remote(sup_in, sup_buf.at[source, 0], sup_send.at[p], sup_recv.at[source], (i, p))

    def row_copy(p, slot):
        return remote(pack.at[z], pack.at[slot], row_send.at[p], row_recv.at[slot], (i, p * CORES + 1 - core))

    loop(0, j, lambda p: dat_copy(p, j).start())
    loop(0, j, answer)
    loop(0, CORES * i, answer_plane)

    for load in loads[:4]:
        load.wait()
    pack[z, :n_rows] = (block_ref[...] * SUP_DEV + offset_ref[...]).astype(jnp.float32)
    pack[z, n_rows : 2 * n_rows] = date_ref[...].astype(jnp.float32)
    pack[z, 2 * n_rows :] = rev_ref[...].astype(jnp.float32)
    loop(0, jnp.minimum(z, 1), lambda p: row_copy(p, z).start())

    for load in loads[4:]:
        load.wait()

    def to_later(p):
        pl.semaphore_wait(ready.at[p], 1)
        dat_copy(p, j).start()

        @pl.when(p % CORES != core)
        def _():
            row_copy(p // CORES, jnp.where(p // CORES == z, Z, z)).start()

    loop(0, j, lambda p: sup_copy(p, j).start())

    cand = cand_ref[...]
    groups = cand.shape[0]
    c_owner = lax.shift_right_logical(cand, 11)
    c_off = cand & (SUP_DEV - 1)
    c_line = c_owner * GROUP + (lax.shift_right_logical(c_off, 7) & (GROUP - 1))
    c_col = lax.shift_right_logical(c_off, 10) * LANES + (c_off & (LANES - 1))
    iota = lax.broadcasted_iota(jnp.int32, (WIDE, LANES), 0)
    for g in range(groups):
        hit = iota == c_col[g : g + 1, :]
        hot[:, g * LANES : (g + 1) * LANES] = jnp.where(hit, 1.0, 0.0).astype(jnp.bfloat16)

    loop(j + 1, C, to_later)
    loop(1, z, lambda p: row_copy(p, z).start())
    loop(j + 1, C, lambda p: sup_copy(p, j).start())

    def others(n, me, body):
        loop(0, me, body)
        loop(me + 1, n, body)

    others(C, j, lambda p: dat_copy(p, p).wait_recv())
    table = jnp.concatenate(
        [dat_buf[c] for c in range(C)] + [jnp.zeros((1, LANES - C * dat_in.shape[1]), jnp.int32)], axis=1
    )

    short = iota.astype(jnp.int16)
    one, nought = jnp.ones((), jnp.bfloat16), jnp.zeros((), jnp.bfloat16)

    def spread(x, r):
        return jnp.broadcast_to(x[r : r + 1, :], (WIDE, LANES))

    def add_rows(source, base, total):
        ids = pack[source, :n_rows].astype(jnp.int32)
        day = pack[source, n_rows : 2 * n_rows].astype(jnp.int32)
        day_word = div_bits(day)
        lit = lax.shift_right_logical(lookup(table, day_word), day - day_word * BITS) & 1
        value = jnp.where(lit == 1, pack[source, 2 * n_rows :], 0.0)
        line = lax.shift_right_logical(ids, 11) * GROUP + (lax.shift_right_logical(ids, 7) & (GROUP - 1)) - base
        column = (lax.shift_right_logical(ids, 10) & 1) * LANES + (ids & (LANES - 1))
        for r in range(0, n_rows, SLAB):
            left = [
                jnp.where(
                    short == spread(line, n).astype(jnp.int16), spread(value, n).astype(jnp.bfloat16), nought
                )[:tall]
                for n in range(r, min(r + SLAB, n_rows))
            ]
            right = [
                jnp.where(short == spread(column, n).astype(jnp.int16), one, nought)
                for n in range(r, min(r + SLAB, n_rows))
            ]
            total = total + lax.dot_general(
                jnp.concatenate(left, axis=1), jnp.concatenate(right, axis=1), (((1,), (1,)), ((), ())),
                preferred_element_type=jnp.float32,
            )
        return total

    def candidates_of(total, base):
        first = total.astype(jnp.bfloat16)
        second = (total - first.astype(jnp.float32)).astype(jnp.bfloat16)
        found = jnp.dot(first, hot[...], preferred_element_type=jnp.float32)
        found = found + jnp.dot(second, hot[...], preferred_element_type=jnp.float32)
        picked = []
        for g in range(groups):
            hit = iota[:tall] == c_line[g : g + 1, :] - base
            picked.append(jnp.sum(jnp.where(hit, found[:, g * LANES : (g + 1) * LANES], 0.0), axis=0, keepdims=True))
        return jnp.concatenate(picked, axis=0)

    empty = jnp.zeros((tall, WIDE), jnp.float32)
    if lines == tall:
        sources = [lax.rem(z + k, Z) for k in range(1, Z)]

        def add_all(total, *batches):
            for batch in batches:
                for slot in batch:
                    if slot is not z:
                        row_copy(z, slot).wait_recv()
                for slot in batch:
                    total = add_rows(slot, 0, total)
            hist[...] = total

        @pl.when(core == 0)
        def _():
            add_all(empty, sources)

        @pl.when(core == 1)
        def _():
            add_all(empty, [z, Z] + sources)

    else:
        others(Z, z, lambda p: row_copy(p, p).wait_recv())
        loop(0, core, lambda n: row_copy(z, Z).wait_recv())

        def fill(t, carry):
            base = pl.multiple_of(t * tall, tall)

            def add(slot, acc):
                return add_rows(slot, base, acc)

            acc = lax.fori_loop(0, z, add, empty)
            acc = lax.fori_loop(z + 1, Z, add, acc)
            hist[pl.ds(base, tall), :] = lax.fori_loop(0, CORES * core, lambda n, a: add(z + n * (Z - z), a), acc)
            return carry

        lax.fori_loop(0, lines // tall, fill, 0)

    plane = [lax.rem(q + k, Q) for k in range(1, Q)]

    @pl.when(i < R - 1)
    def _():
        pl.semaphore_wait(ready_plane, CORES * (R - 1 - i))

    def lines_of(p):
        owner = (p // CORES) * C + z * CORES + p % CORES
        return hist.at[pl.ds(pl.multiple_of(owner * GROUP, GROUP), GROUP), :]

    h_copies = [
        remote(lines_of(p), part.at[k], h_send.at[k], h_recv.at[k], at_plane(p)) for k, p in enumerate(plane)
    ]
    for copy in h_copies:
        copy.start()

    if lines == tall:
        mine = candidates_of(hist[...], 0)
    else:

        def gather(t, acc):
            base = pl.multiple_of(t * tall, tall)
            return acc + candidates_of(hist[pl.ds(base, tall), :], base)

        mine = lax.fori_loop(0, lines // tall, gather, jnp.zeros(cand.shape, jnp.float32))
    cpart[...] = mine
    c_copies = [
        remote(cpart, cparts.at[k], c_send.at[k], c_recv.at[k], at_plane(p)) for k, p in enumerate(plane)
    ]
    for copy in c_copies:
        copy.start()

    others(C, j, lambda p: sup_copy(p, p).wait_recv())
    full = n_words // LANES

    def words_at(source, flat):
        word = lookup(sup_buf[source, :, n_words - LANES :], jnp.maximum(flat - (n_words - LANES), 0))
        for t in range(full):
            near = (flat >= t * LANES) & (flat < (t + 1) * LANES)
            word = jnp.where(near, lookup(sup_buf[source, :, t * LANES : (t + 1) * LANES], flat & (LANES - 1)), word)
        return word

    c_word = div_bits(c_off)
    c_bit = c_off - c_word * BITS
    c_source = lax.div(c_owner, R)
    c_flat = (c_owner - c_source * R) * per_block + c_word

    def word_of(source, acc):
        return jnp.where(c_source == source, words_at(source, c_flat), acc)

    c_words = lax.fori_loop(0, C, word_of, jnp.zeros(cand.shape, jnp.int32))
    c_lit = (lax.shift_right_logical(c_words, c_bit) & 1) == 1

    me = i * C + j
    shape = (owned_rows, LANES)
    spot = lax.broadcasted_iota(jnp.int32, shape, 0) * LANES + lax.broadcasted_iota(jnp.int32, shape, 1)
    spot_word = div_bits(spot)
    my_words = words_at(me // R, lax.rem(me, R) * per_block + spot_word)
    my_lit = (lax.shift_right_logical(my_words, spot - spot_word * BITS) & 1) == 1

    owned = hist[pl.ds(pl.multiple_of(me * GROUP, GROUP), GROUP), :]
    for k, copy in enumerate(h_copies):
        copy.wait_recv()
        owned = owned + part[k]
    both_ref[:GROUP, :] = jnp.where(my_lit[:GROUP], owned[:, :LANES], 0.0)
    both_ref[GROUP:owned_rows, :] = jnp.where(my_lit[GROUP:], owned[:, LANES:], 0.0)

    found = cpart[...]
    for k, copy in enumerate(c_copies):
        copy.wait_recv()
        found = found + cparts[k]
    both_ref[owned_rows:, :] = jnp.where(c_lit, found, 0.0)

    others(C, j, lambda p: dat_copy(p, j).wait_send())
    others(C, j, lambda p: sup_copy(p, j).wait_send())
    others(Z, z, lambda p: row_copy(p, z).wait_send())
    loop(core, 1, lambda n: row_copy(z, Z).wait_send())
    for copy in h_copies + c_copies:
        copy.wait_send()


def in_hbm(x):
    return pltpu.with_memory_space_constraint(x, pltpu.HBM)


def finish(both_ref, owned_ref, cand_out_ref, total_ref):
    owned_rows = owned_ref.shape[0]
    owned_ref[...] = both_ref[:owned_rows, :]
    found = both_ref[owned_rows:, :]
    cand_out_ref[...] = found
    total_ref[0, 0] = jnp.sum(found)


def per_device(R, C, fact_block, fact_offset, fact_date, revenue, supplier_words, date_words, candidates):
    rows = fact_offset.shape[0] // LANES
    cands = candidates.shape[0] // LANES
    Z, Q = C // CORES, R * CORES
    f32, i32 = jnp.float32, jnp.int32
    dma = pltpu.SemaphoreType.DMA
    vmem = pl.BlockSpec(memory_space=pltpu.VMEM)
    both = pl.pallas_call(
        functools.partial(kernel, R, C),
        out_shape=jax.ShapeDtypeStruct((SUP_DEV // LANES + cands, LANES), f32),
        in_specs=[pl.BlockSpec(memory_space=pl.ANY)] * 7,
        out_specs=vmem,
        scratch_shapes=[
            pltpu.VMEM((rows, LANES), i32),
            pltpu.VMEM((rows, LANES), i32),
            pltpu.VMEM((rows, LANES), i32),
            pltpu.VMEM((rows, LANES), revenue.dtype),
            pltpu.VMEM((cands, LANES), i32),
            dma((7,)),
            pltpu.VMEM((Z + 1, 3 * rows, LANES), f32),
            pltpu.VMEM((WIDE, cands * LANES), jnp.bfloat16),
            pltpu.VMEM((R * C * GROUP, WIDE), f32),
            pltpu.VMEM((C, 1, date_words.shape[0]), i32),
            pltpu.VMEM((C, 1, supplier_words.shape[0]), i32),
            pltpu.VMEM((Q - 1, GROUP, WIDE), f32),
            pltpu.VMEM((cands, LANES), f32),
            pltpu.VMEM((Q - 1, cands, LANES), f32),
            pltpu.SemaphoreType.REGULAR((C,)),
            pltpu.SemaphoreType.REGULAR,
            dma((C,)), dma((C,)), dma((C,)), dma((C,)), dma((Z,)), dma((Z + 1,)),
            dma((Q - 1,)), dma((Q - 1,)), dma((Q - 1,)), dma((Q - 1,)),
        ],
        compiler_params=pltpu.CompilerParams(
            collective_id=0, has_side_effects=True, vmem_limit_bytes=KERNEL_VMEM
        ),
        name="revenue",
    )(
        in_hbm(fact_block.reshape(rows, LANES)),
        in_hbm(fact_offset.reshape(rows, LANES)),
        in_hbm(fact_date.reshape(rows, LANES)),
        in_hbm(revenue.reshape(rows, LANES)),
        in_hbm(candidates.reshape(cands, LANES)),
        in_hbm(supplier_words),
        in_hbm(date_words.reshape(1, -1)),
    )
    owned, found, total = pl.pallas_call(
        finish,
        out_shape=(
            jax.ShapeDtypeStruct((SUP_DEV // LANES, LANES), f32),
            jax.ShapeDtypeStruct((cands, LANES), f32),
            jax.ShapeDtypeStruct((1, 1), f32),
        ),
        in_specs=[vmem],
        out_specs=(vmem, vmem, pl.BlockSpec(memory_space=pltpu.SMEM)),
        compiler_params=pltpu.CompilerParams(vmem_limit_bytes=FINISH_VMEM),
        name="finish",
    )(both)
    return owned.reshape(SUP_DEV), found.reshape(candidates.shape), total.reshape(())


def solution(mesh):
    in_specs = (
        P(("row", "col"), None),
        P(("row", "col")),
        P(("row", "col")),
        P(("row", "col")),
        P("col"),
        P("col"),
        P(),
    )
    out_specs = (P(("row", "col")), P(), P())
    body = functools.partial(per_device, mesh.shape["row"], mesh.shape["col"])
    return jax.shard_map(body, mesh=mesh, in_specs=in_specs, out_specs=out_specs, check_vma=False)
```

```python
import functools

import jax
import jax.numpy as jnp
from jax import lax
from jax.experimental import pallas as pl
from jax.experimental.pallas import tpu as pltpu
from jax.sharding import PartitionSpec as P

SUP_DEV = 2048
LANES = 128
WIDE = 2 * LANES
GROUP = SUP_DEV // WIDE
BITS = 30
CORES = 2
SLAB = 4
KERNEL_VMEM = 40 << 20
FINISH_VMEM = 1 << 20
MESH = pl.DeviceIdType.MESH


def div_bits(x):
    return lax.shift_right_logical(x * 2185, 16)


def lookup(row, index):
    table = jnp.broadcast_to(row, index.shape)
    return jnp.take_along_axis(table, index, axis=1, mode="promise_in_bounds")


def kernel(
    rows_axis, cols_axis,
    block_in, offset_in, date_in, rev_in, cand_in, sup_in, dat_in,
    both_ref,
    block_ref, offset_ref, date_ref, rev_ref, cand_ref, load_sem,
    pack, hot, hist, dat_buf, sup_buf, part, cpart, cparts,
    ready, ready_plane, dat_send, dat_recv, sup_send, sup_recv, row_send, row_recv,
    h_send, h_recv, c_send, c_recv,
):
    R, C = rows_axis, cols_axis
    Z, Q = C // CORES, R * CORES
    i, j = lax.axis_index("row"), lax.axis_index("col")
    z, core = j // CORES, j % CORES
    q = i * CORES + core
    n_rows = block_ref.shape[0]
    n_words = sup_in.shape[0]
    per_block = n_words // R
    owned_rows = both_ref.shape[0] - cand_ref.shape[0]
    lines = R * C * GROUP
    tall = min(lines, WIDE)

    pairs = [
        (offset_in, offset_ref), (block_in, block_ref), (date_in, date_ref), (rev_in, rev_ref),
        (cand_in, cand_ref), (dat_in, dat_buf.at[j]), (sup_in, sup_buf.at[j, 0]),
    ]
    loads = [pltpu.make_async_copy(src, dst, load_sem.at[n]) for n, (src, dst) in enumerate(pairs)]
    for load in loads:
        load.start()

    barrier = pltpu.get_barrier_semaphore()

    def loop(low, high, body):
        def step(n, carry):
            body(n)
            return carry

        lax.fori_loop(low, high, step, 0)

    def at_plane(p):
        return (p // CORES, z * CORES + p % CORES)

    def greet(peer):
        pl.semaphore_signal(barrier, inc=1, device_id=peer, device_id_type=MESH)

    loop(j + 1, C, lambda p: greet((i, p)))
    loop(CORES * (i + 1), Q, lambda p: greet(at_plane(p)))

    @pl.when(j + CORES * i > 0)
    def _():
        pl.semaphore_wait(barrier, j + CORES * i)

    def answer(p):
        pl.semaphore_signal(ready.at[j], inc=1, device_id=(i, p), device_id_type=MESH)

    def answer_plane(p):
        pl.semaphore_signal(ready_plane, inc=1, device_id=at_plane(p), device_id_type=MESH)

    def remote(src, dst, send, recv, peer):
        return pltpu.make_async_remote_copy(
            src_ref=src, dst_ref=dst, send_sem=send, recv_sem=recv, device_id=peer, device_id_type=MESH
        )

    def dat_copy(p, source):
        return remote(dat_in, dat_buf.at[source], dat_send.at[p], dat_recv.at[source], (i, p))

    def sup_copy(p, source):
        return remote(sup_in, sup_buf.at[source, 0], sup_send.at[p], sup_recv.at[source], (i, p))

    def row_copy(p, slot):
        return remote(pack.at[z], pack.at[slot], row_send.at[p], row_recv.at[slot], (i, p * CORES + 1 - core))

    loop(0, j, lambda p: dat_copy(p, j).start())
    loop(0, j, answer)
    loop(0, CORES * i, answer_plane)

    for load in loads[:4]:
        load.wait()
    pack[z, :n_rows] = (block_ref[...] * SUP_DEV + offset_ref[...]).astype(jnp.float32)
    pack[z, n_rows : 2 * n_rows] = date_ref[...].astype(jnp.float32)
    pack[z, 2 * n_rows :] = rev_ref[...].astype(jnp.float32)
    loop(0, jnp.minimum(z, 1), lambda p: row_copy(p, z).start())

    for load in loads[4:]:
        load.wait()

    def to_later(p):
        pl.semaphore_wait(ready.at[p], 1)
        dat_copy(p, j).start()

        @pl.when(p % CORES != core)
        def _():
            row_copy(p // CORES, jnp.where(p // CORES == z, Z, z)).start()

    loop(0, j, lambda p: sup_copy(p, j).start())

    cand = cand_ref[...]
    groups = cand.shape[0]
    c_owner = lax.shift_right_logical(cand, 11)
    c_off = cand & (SUP_DEV - 1)
    c_line = c_owner * GROUP + (lax.shift_right_logical(c_off, 7) & (GROUP - 1))
    c_col = lax.shift_right_logical(c_off, 10) * LANES + (c_off & (LANES - 1))
    iota = lax.broadcasted_iota(jnp.int32, (WIDE, LANES), 0)
    for g in range(groups):
        hit = iota == c_col[g : g + 1, :]
        hot[:, g * LANES : (g + 1) * LANES] = jnp.where(hit, 1.0, 0.0).astype(jnp.bfloat16)

    loop(j + 1, C, to_later)
    loop(1, z, lambda p: row_copy(p, z).start())
    loop(j + 1, C, lambda p: sup_copy(p, j).start())

    def others(n, me, body):
        loop(0, me, body)
        loop(me + 1, n, body)

    others(C, j, lambda p: dat_copy(p, p).wait_recv())
    table = jnp.concatenate(
        [dat_buf[c] for c in range(C)] + [jnp.zeros((1, LANES - C * dat_in.shape[1]), jnp.int32)], axis=1
    )

    short = iota.astype(jnp.int16)
    one, nought = jnp.ones((), jnp.bfloat16), jnp.zeros((), jnp.bfloat16)

    def spread(x, r):
        return jnp.broadcast_to(x[r : r + 1, :], (WIDE, LANES))

    def add_rows(source, base, total, low=0, high=n_rows):
        ids = pack[source, :n_rows].astype(jnp.int32)
        day = pack[source, n_rows : 2 * n_rows].astype(jnp.int32)
        day_word = div_bits(day)
        lit = lax.shift_right_logical(lookup(table, day_word), day - day_word * BITS) & 1
        value = jnp.where(lit == 1, pack[source, 2 * n_rows :], 0.0)
        line = lax.shift_right_logical(ids, 11) * GROUP + (lax.shift_right_logical(ids, 7) & (GROUP - 1)) - base
        column = (lax.shift_right_logical(ids, 10) & 1) * LANES + (ids & (LANES - 1))
        for r in range(low, high, SLAB):
            left = [
                jnp.where(
                    short == spread(line, n).astype(jnp.int16), spread(value, n).astype(jnp.bfloat16), nought
                )[:tall]
                for n in range(r, min(r + SLAB, high))
            ]
            right = [
                jnp.where(short == spread(column, n).astype(jnp.int16), one, nought)
                for n in range(r, min(r + SLAB, high))
            ]
            total = total + lax.dot_general(
                jnp.concatenate(left, axis=1), jnp.concatenate(right, axis=1), (((1,), (1,)), ((), ())),
                preferred_element_type=jnp.float32,
            )
        return total

    def candidates_of(total, base):
        first = total.astype(jnp.bfloat16)
        second = (total - first.astype(jnp.float32)).astype(jnp.bfloat16)
        found = jnp.dot(first, hot[...], preferred_element_type=jnp.float32)
        found = found + jnp.dot(second, hot[...], preferred_element_type=jnp.float32)
        picked = []
        for g in range(groups):
            hit = iota[:tall] == c_line[g : g + 1, :] - base
            picked.append(jnp.sum(jnp.where(hit, found[:, g * LANES : (g + 1) * LANES], 0.0), axis=0, keepdims=True))
        return jnp.concatenate(picked, axis=0)

    empty = jnp.zeros((tall, WIDE), jnp.float32)
    if lines == tall:
        sources = [lax.rem(z + k, Z) for k in range(1, Z)]

        def wait(slots):
            for slot in slots:
                row_copy(z, slot).wait_recv()

        share = n_rows * 2 // 3 // SLAB * SLAB

        @pl.when(core == 0)
        def _():
            wait(sources)
            total = add_rows(z, 0, empty, 0, share)
            for slot in sources:
                total = add_rows(slot, 0, total)
            hist[...] = total

        @pl.when(core == 1)
        def _():
            wait([Z] + sources)
            total = add_rows(z, 0, add_rows(Z, 0, empty, share))
            for slot in sources:
                total = add_rows(slot, 0, total)
            hist[...] = total

    else:
        others(Z, z, lambda p: row_copy(p, p).wait_recv())
        loop(0, core, lambda n: row_copy(z, Z).wait_recv())

        def fill(t, carry):
            base = pl.multiple_of(t * tall, tall)

            def add(slot, acc):
                return add_rows(slot, base, acc)

            acc = lax.fori_loop(0, z, add, empty)
            acc = lax.fori_loop(z + 1, Z, add, acc)
            hist[pl.ds(base, tall), :] = lax.fori_loop(0, CORES * core, lambda n, a: add(z + n * (Z - z), a), acc)
            return carry

        lax.fori_loop(0, lines // tall, fill, 0)

    plane = [lax.rem(q + k, Q) for k in range(1, Q)]

    @pl.when(i < R - 1)
    def _():
        pl.semaphore_wait(ready_plane, CORES * (R - 1 - i))

    def lines_of(p):
        owner = (p // CORES) * C + z * CORES + p % CORES
        return hist.at[pl.ds(pl.multiple_of(owner * GROUP, GROUP), GROUP), :]

    h_copies = [
        remote(lines_of(p), part.at[k], h_send.at[k], h_recv.at[k], at_plane(p)) for k, p in enumerate(plane)
    ]
    for copy in h_copies:
        copy.start()

    if lines == tall:
        mine = candidates_of(hist[...], 0)
    else:

        def gather(t, acc):
            base = pl.multiple_of(t * tall, tall)
            return acc + candidates_of(hist[pl.ds(base, tall), :], base)

        mine = lax.fori_loop(0, lines // tall, gather, jnp.zeros(cand.shape, jnp.float32))
    cpart[...] = mine
    c_copies = [
        remote(cpart, cparts.at[k], c_send.at[k], c_recv.at[k], at_plane(p)) for k, p in enumerate(plane)
    ]
    for copy in c_copies:
        copy.start()

    others(C, j, lambda p: sup_copy(p, p).wait_recv())
    full = n_words // LANES

    def words_at(source, flat):
        word = lookup(sup_buf[source, :, n_words - LANES :], jnp.maximum(flat - (n_words - LANES), 0))
        for t in range(full):
            near = (flat >= t * LANES) & (flat < (t + 1) * LANES)
            word = jnp.where(near, lookup(sup_buf[source, :, t * LANES : (t + 1) * LANES], flat & (LANES - 1)), word)
        return word

    c_word = div_bits(c_off)
    c_bit = c_off - c_word * BITS
    c_source = lax.div(c_owner, R)
    c_flat = (c_owner - c_source * R) * per_block + c_word

    def word_of(source, acc):
        return jnp.where(c_source == source, words_at(source, c_flat), acc)

    c_words = lax.fori_loop(0, C, word_of, jnp.zeros(cand.shape, jnp.int32))
    c_lit = (lax.shift_right_logical(c_words, c_bit) & 1) == 1

    me = i * C + j
    shape = (owned_rows, LANES)
    spot = lax.broadcasted_iota(jnp.int32, shape, 0) * LANES + lax.broadcasted_iota(jnp.int32, shape, 1)
    spot_word = div_bits(spot)
    my_words = words_at(me // R, lax.rem(me, R) * per_block + spot_word)
    my_lit = (lax.shift_right_logical(my_words, spot - spot_word * BITS) & 1) == 1

    owned = hist[pl.ds(pl.multiple_of(me * GROUP, GROUP), GROUP), :]
    for k, copy in enumerate(h_copies):
        copy.wait_recv()
        owned = owned + part[k]
    both_ref[:GROUP, :] = jnp.where(my_lit[:GROUP], owned[:, :LANES], 0.0)
    both_ref[GROUP:owned_rows, :] = jnp.where(my_lit[GROUP:], owned[:, LANES:], 0.0)

    found = cpart[...]
    for k, copy in enumerate(c_copies):
        copy.wait_recv()
        found = found + cparts[k]
    both_ref[owned_rows:, :] = jnp.where(c_lit, found, 0.0)

    others(C, j, lambda p: dat_copy(p, j).wait_send())
    others(C, j, lambda p: sup_copy(p, j).wait_send())
    others(Z, z, lambda p: row_copy(p, z).wait_send())
    loop(core, 1, lambda n: row_copy(z, Z).wait_send())
    for copy in h_copies + c_copies:
        copy.wait_send()


def in_hbm(x):
    return pltpu.with_memory_space_constraint(x, pltpu.HBM)


def finish(both_ref, owned_ref, cand_out_ref, total_ref):
    owned_rows = owned_ref.shape[0]
    owned_ref[...] = both_ref[:owned_rows, :]
    found = both_ref[owned_rows:, :]
    cand_out_ref[...] = found
    total_ref[0, 0] = jnp.sum(found)


def per_device(R, C, fact_block, fact_offset, fact_date, revenue, supplier_words, date_words, candidates):
    rows = fact_offset.shape[0] // LANES
    cands = candidates.shape[0] // LANES
    Z, Q = C // CORES, R * CORES
    f32, i32 = jnp.float32, jnp.int32
    dma = pltpu.SemaphoreType.DMA
    vmem = pl.BlockSpec(memory_space=pltpu.VMEM)
    both = pl.pallas_call(
        functools.partial(kernel, R, C),
        out_shape=jax.ShapeDtypeStruct((SUP_DEV // LANES + cands, LANES), f32),
        in_specs=[pl.BlockSpec(memory_space=pl.ANY)] * 7,
        out_specs=vmem,
        scratch_shapes=[
            pltpu.VMEM((rows, LANES), i32),
            pltpu.VMEM((rows, LANES), i32),
            pltpu.VMEM((rows, LANES), i32),
            pltpu.VMEM((rows, LANES), revenue.dtype),
            pltpu.VMEM((cands, LANES), i32),
            dma((7,)),
            pltpu.VMEM((Z + 1, 3 * rows, LANES), f32),
            pltpu.VMEM((WIDE, cands * LANES), jnp.bfloat16),
            pltpu.VMEM((R * C * GROUP, WIDE), f32),
            pltpu.VMEM((C, 1, date_words.shape[0]), i32),
            pltpu.VMEM((C, 1, supplier_words.shape[0]), i32),
            pltpu.VMEM((Q - 1, GROUP, WIDE), f32),
            pltpu.VMEM((cands, LANES), f32),
            pltpu.VMEM((Q - 1, cands, LANES), f32),
            pltpu.SemaphoreType.REGULAR((C,)),
            pltpu.SemaphoreType.REGULAR,
            dma((C,)), dma((C,)), dma((C,)), dma((C,)), dma((Z,)), dma((Z + 1,)),
            dma((Q - 1,)), dma((Q - 1,)), dma((Q - 1,)), dma((Q - 1,)),
        ],
        compiler_params=pltpu.CompilerParams(
            collective_id=0, has_side_effects=True, vmem_limit_bytes=KERNEL_VMEM
        ),
        name="revenue",
    )(
        in_hbm(fact_block.reshape(rows, LANES)),
        in_hbm(fact_offset.reshape(rows, LANES)),
        in_hbm(fact_date.reshape(rows, LANES)),
        in_hbm(revenue.reshape(rows, LANES)),
        in_hbm(candidates.reshape(cands, LANES)),
        in_hbm(supplier_words),
        in_hbm(date_words.reshape(1, -1)),
    )
    owned, found, total = pl.pallas_call(
        finish,
        out_shape=(
            jax.ShapeDtypeStruct((SUP_DEV // LANES, LANES), f32),
            jax.ShapeDtypeStruct((cands, LANES), f32),
            jax.ShapeDtypeStruct((1, 1), f32),
        ),
        in_specs=[vmem],
        out_specs=(vmem, vmem, pl.BlockSpec(memory_space=pltpu.SMEM)),
        compiler_params=pltpu.CompilerParams(vmem_limit_bytes=FINISH_VMEM),
        name="finish",
    )(both)
    return owned.reshape(SUP_DEV), found.reshape(candidates.shape), total.reshape(())


def solution(mesh):
    in_specs = (
        P(("row", "col"), None),
        P(("row", "col")),
        P(("row", "col")),
        P(("row", "col")),
        P("col"),
        P("col"),
        P(),
    )
    out_specs = (P(("row", "col")), P(), P())
    body = functools.partial(per_device, mesh.shape["row"], mesh.shape["col"])
    return jax.shard_map(body, mesh=mesh, in_specs=in_specs, out_specs=out_specs, check_vma=False)
```

```python
import functools

import jax
import jax.numpy as jnp
from jax import lax
from jax.experimental import pallas as pl
from jax.experimental.pallas import tpu as pltpu
from jax.sharding import PartitionSpec as P

SUP_DEV = 2048
LANES = 128
WIDE = 2 * LANES
GROUP = SUP_DEV // WIDE
BITS = 30
CORES = 2
SLAB = 4
KERNEL_VMEM = 40 << 20
FINISH_VMEM = 1 << 20
MESH = pl.DeviceIdType.MESH


def div_bits(x):
    return lax.shift_right_logical(x * 2185, 16)


def lookup(row, index):
    table = jnp.broadcast_to(row, index.shape)
    return jnp.take_along_axis(table, index, axis=1, mode="promise_in_bounds")


def kernel(
    rows_axis, cols_axis,
    block_in, offset_in, date_in, rev_in, cand_in, sup_in, dat_in,
    both_ref,
    block_ref, offset_ref, date_ref, rev_ref, cand_ref, load_sem,
    pack, hot, hist, dat_buf, sup_buf, part, cpart, cparts,
    ready, ready_plane, dat_send, dat_recv, sup_send, sup_recv, row_send, row_recv,
    h_send, h_recv, c_send, c_recv,
):
    R, C = rows_axis, cols_axis
    Z, Q = C // CORES, R * CORES
    i, j = lax.axis_index("row"), lax.axis_index("col")
    z, core = j // CORES, j % CORES
    q = i * CORES + core
    n_rows = block_ref.shape[0]
    n_words = sup_in.shape[0]
    per_block = n_words // R
    owned_rows = both_ref.shape[0] - cand_ref.shape[0]
    lines = R * C * GROUP
    tall = min(lines, WIDE)

    pairs = [
        (offset_in, offset_ref), (block_in, block_ref), (date_in, date_ref), (rev_in, rev_ref),
        (cand_in, cand_ref), (dat_in, dat_buf.at[j]), (sup_in, sup_buf.at[j, 0]),
    ]
    loads = [pltpu.make_async_copy(src, dst, load_sem.at[n]) for n, (src, dst) in enumerate(pairs)]
    for load in loads:
        load.start()

    barrier = pltpu.get_barrier_semaphore()

    def loop(low, high, body):
        def step(n, carry):
            body(n)
            return carry

        lax.fori_loop(low, high, step, 0)

    def at_plane(p):
        return (p // CORES, z * CORES + p % CORES)

    def greet(peer):
        pl.semaphore_signal(barrier, inc=1, device_id=peer, device_id_type=MESH)

    loop(j + 1, C, lambda p: greet((i, p)))
    loop(CORES * (i + 1), Q, lambda p: greet(at_plane(p)))

    @pl.when(j + CORES * i > 0)
    def _():
        pl.semaphore_wait(barrier, j + CORES * i)

    def answer(p):
        pl.semaphore_signal(ready.at[j], inc=1, device_id=(i, p), device_id_type=MESH)

    def answer_plane(p):
        pl.semaphore_signal(ready_plane, inc=1, device_id=at_plane(p), device_id_type=MESH)

    def remote(src, dst, send, recv, peer):
        return pltpu.make_async_remote_copy(
            src_ref=src, dst_ref=dst, send_sem=send, recv_sem=recv, device_id=peer, device_id_type=MESH
        )

    def dat_copy(p, source):
        return remote(dat_in, dat_buf.at[source], dat_send.at[p], dat_recv.at[source], (i, p))

    def sup_copy(p, source):
        return remote(sup_in, sup_buf.at[source, 0], sup_send.at[p], sup_recv.at[source], (i, p))

    def row_copy(p, slot):
        return remote(pack.at[z], pack.at[slot], row_send.at[p], row_recv.at[slot], (i, p * CORES + 1 - core))

    loop(0, j, lambda p: dat_copy(p, j).start())
    loop(0, j, answer)
    loop(0, CORES * i, answer_plane)

    for load in loads[:4]:
        load.wait()
    pack[z, :n_rows] = (block_ref[...] * SUP_DEV + offset_ref[...]).astype(jnp.float32)
    pack[z, n_rows : 2 * n_rows] = date_ref[...].astype(jnp.float32)
    pack[z, 2 * n_rows :] = rev_ref[...].astype(jnp.float32)
    loop(0, jnp.minimum(z, 1), lambda p: row_copy(p, z).start())

    for load in loads[4:]:
        load.wait()

    def to_later(p):
        pl.semaphore_wait(ready.at[p], 1)
        dat_copy(p, j).start()

        @pl.when(p % CORES != core)
        def _():
            row_copy(p // CORES, jnp.where(p // CORES == z, Z, z)).start()

    loop(0, j, lambda p: sup_copy(p, j).start())

    cand = cand_ref[...]
    groups = cand.shape[0]
    c_owner = lax.shift_right_logical(cand, 11)
    c_off = cand & (SUP_DEV - 1)
    c_line = c_owner * GROUP + (lax.shift_right_logical(c_off, 7) & (GROUP - 1))
    c_col = lax.shift_right_logical(c_off, 10) * LANES + (c_off & (LANES - 1))
    iota = lax.broadcasted_iota(jnp.int32, (WIDE, LANES), 0)
    for g in range(groups):
        hit = iota == c_col[g : g + 1, :]
        hot[:, g * LANES : (g + 1) * LANES] = jnp.where(hit, 1.0, 0.0).astype(jnp.bfloat16)

    loop(j + 1, C, to_later)
    loop(j + 1, C, lambda p: sup_copy(p, j).start())
    loop(CORES * (z + 1), C, lambda p: dat_copy(p, p).wait_recv())
    loop(1, z, lambda p: row_copy(p, z).start())

    def others(n, me, body):
        loop(0, me, body)
        loop(me + 1, n, body)

    others(CORES * (z + 1), j, lambda p: dat_copy(p, p).wait_recv())
    table = jnp.concatenate(
        [dat_buf[c] for c in range(C)] + [jnp.zeros((1, LANES - C * dat_in.shape[1]), jnp.int32)], axis=1
    )

    short = iota.astype(jnp.int16)
    one, nought = jnp.ones((), jnp.bfloat16), jnp.zeros((), jnp.bfloat16)

    def spread(x, r):
        return jnp.broadcast_to(x[r : r + 1, :], (WIDE, LANES))

    def add_rows(source, base, total, low=0, high=n_rows):
        ids = pack[source, :n_rows].astype(jnp.int32)
        day = pack[source, n_rows : 2 * n_rows].astype(jnp.int32)
        day_word = div_bits(day)
        lit = lax.shift_right_logical(lookup(table, day_word), day - day_word * BITS) & 1
        value = jnp.where(lit == 1, pack[source, 2 * n_rows :], 0.0)
        line = lax.shift_right_logical(ids, 11) * GROUP + (lax.shift_right_logical(ids, 7) & (GROUP - 1)) - base
        column = (lax.shift_right_logical(ids, 10) & 1) * LANES + (ids & (LANES - 1))
        for r in range(low, high, SLAB):
            left = [
                jnp.where(
                    short == spread(line, n).astype(jnp.int16), spread(value, n).astype(jnp.bfloat16), nought
                )[:tall]
                for n in range(r, min(r + SLAB, high))
            ]
            right = [
                jnp.where(short == spread(column, n).astype(jnp.int16), one, nought)
                for n in range(r, min(r + SLAB, high))
            ]
            total = total + lax.dot_general(
                jnp.concatenate(left, axis=1), jnp.concatenate(right, axis=1), (((1,), (1,)), ((), ())),
                preferred_element_type=jnp.float32,
            )
        return total

    def candidates_of(total, base):
        first = total.astype(jnp.bfloat16)
        second = (total - first.astype(jnp.float32)).astype(jnp.bfloat16)
        found = jnp.dot(first, hot[...], preferred_element_type=jnp.float32)
        found = found + jnp.dot(second, hot[...], preferred_element_type=jnp.float32)
        picked = []
        for g in range(groups):
            hit = iota[:tall] == c_line[g : g + 1, :] - base
            picked.append(jnp.sum(jnp.where(hit, found[:, g * LANES : (g + 1) * LANES], 0.0), axis=0, keepdims=True))
        return jnp.concatenate(picked, axis=0)

    empty = jnp.zeros((tall, WIDE), jnp.float32)
    if lines == tall:
        sources = [lax.rem(z + k, Z) for k in range(1, Z)]

        def wait(slots):
            for slot in slots:
                row_copy(z, slot).wait_recv()

        share = n_rows * 2 // 3 // SLAB * SLAB

        @pl.when(core == 0)
        def _():
            wait(sources)
            total = add_rows(z, 0, empty, 0, share)
            for slot in sources:
                total = add_rows(slot, 0, total)
            hist[...] = total

        @pl.when(core == 1)
        def _():
            wait([Z] + sources)
            total = add_rows(z, 0, add_rows(Z, 0, empty, share))
            for slot in sources:
                total = add_rows(slot, 0, total)
            hist[...] = total

    else:
        others(Z, z, lambda p: row_copy(p, p).wait_recv())
        loop(0, core, lambda n: row_copy(z, Z).wait_recv())

        def fill(t, carry):
            base = pl.multiple_of(t * tall, tall)

            def add(slot, acc):
                return add_rows(slot, base, acc)

            acc = lax.fori_loop(0, z, add, empty)
            acc = lax.fori_loop(z + 1, Z, add, acc)
            hist[pl.ds(base, tall), :] = lax.fori_loop(0, CORES * core, lambda n, a: add(z + n * (Z - z), a), acc)
            return carry

        lax.fori_loop(0, lines // tall, fill, 0)

    plane = [lax.rem(q + k, Q) for k in range(1, Q)]

    @pl.when(i < R - 1)
    def _():
        pl.semaphore_wait(ready_plane, CORES * (R - 1 - i))

    def lines_of(p):
        owner = (p // CORES) * C + z * CORES + p % CORES
        return hist.at[pl.ds(pl.multiple_of(owner * GROUP, GROUP), GROUP), :]

    h_copies = [
        remote(lines_of(p), part.at[k], h_send.at[k], h_recv.at[k], at_plane(p)) for k, p in enumerate(plane)
    ]
    for copy in h_copies:
        copy.start()

    if lines == tall:
        mine = candidates_of(hist[...], 0)
    else:

        def gather(t, acc):
            base = pl.multiple_of(t * tall, tall)
            return acc + candidates_of(hist[pl.ds(base, tall), :], base)

        mine = lax.fori_loop(0, lines // tall, gather, jnp.zeros(cand.shape, jnp.float32))
    cpart[...] = mine
    c_copies = [
        remote(cpart, cparts.at[k], c_send.at[k], c_recv.at[k], at_plane(p)) for k, p in enumerate(plane)
    ]
    for copy in c_copies:
        copy.start()

    others(C, j, lambda p: sup_copy(p, p).wait_recv())
    full = n_words // LANES

    def words_at(source, flat):
        word = lookup(sup_buf[source, :, n_words - LANES :], jnp.maximum(flat - (n_words - LANES), 0))
        for t in range(full):
            near = (flat >= t * LANES) & (flat < (t + 1) * LANES)
            word = jnp.where(near, lookup(sup_buf[source, :, t * LANES : (t + 1) * LANES], flat & (LANES - 1)), word)
        return word

    c_word = div_bits(c_off)
    c_bit = c_off - c_word * BITS
    c_source = lax.div(c_owner, R)
    c_flat = (c_owner - c_source * R) * per_block + c_word

    def word_of(source, acc):
        return jnp.where(c_source == source, words_at(source, c_flat), acc)

    c_words = lax.fori_loop(0, C, word_of, jnp.zeros(cand.shape, jnp.int32))
    c_lit = (lax.shift_right_logical(c_words, c_bit) & 1) == 1

    me = i * C + j
    shape = (owned_rows, LANES)
    spot = lax.broadcasted_iota(jnp.int32, shape, 0) * LANES + lax.broadcasted_iota(jnp.int32, shape, 1)
    spot_word = div_bits(spot)
    my_words = words_at(me // R, lax.rem(me, R) * per_block + spot_word)
    my_lit = (lax.shift_right_logical(my_words, spot - spot_word * BITS) & 1) == 1

    owned = hist[pl.ds(pl.multiple_of(me * GROUP, GROUP), GROUP), :]
    for k, copy in enumerate(h_copies):
        copy.wait_recv()
        owned = owned + part[k]
    both_ref[:GROUP, :] = jnp.where(my_lit[:GROUP], owned[:, :LANES], 0.0)
    both_ref[GROUP:owned_rows, :] = jnp.where(my_lit[GROUP:], owned[:, LANES:], 0.0)

    found = cpart[...]
    for k, copy in enumerate(c_copies):
        copy.wait_recv()
        found = found + cparts[k]
    both_ref[owned_rows:, :] = jnp.where(c_lit, found, 0.0)

    others(C, j, lambda p: dat_copy(p, j).wait_send())
    others(C, j, lambda p: sup_copy(p, j).wait_send())
    others(Z, z, lambda p: row_copy(p, z).wait_send())
    loop(core, 1, lambda n: row_copy(z, Z).wait_send())
    for copy in h_copies + c_copies:
        copy.wait_send()


def in_hbm(x):
    return pltpu.with_memory_space_constraint(x, pltpu.HBM)


def finish(both_ref, owned_ref, cand_out_ref, total_ref):
    owned_rows = owned_ref.shape[0]
    owned_ref[...] = both_ref[:owned_rows, :]
    found = both_ref[owned_rows:, :]
    cand_out_ref[...] = found
    total_ref[0, 0] = jnp.sum(found)


def per_device(R, C, fact_block, fact_offset, fact_date, revenue, supplier_words, date_words, candidates):
    rows = fact_offset.shape[0] // LANES
    cands = candidates.shape[0] // LANES
    Z, Q = C // CORES, R * CORES
    f32, i32 = jnp.float32, jnp.int32
    dma = pltpu.SemaphoreType.DMA
    vmem = pl.BlockSpec(memory_space=pltpu.VMEM)
    both = pl.pallas_call(
        functools.partial(kernel, R, C),
        out_shape=jax.ShapeDtypeStruct((SUP_DEV // LANES + cands, LANES), f32),
        in_specs=[pl.BlockSpec(memory_space=pl.ANY)] * 7,
        out_specs=vmem,
        scratch_shapes=[
            pltpu.VMEM((rows, LANES), i32),
            pltpu.VMEM((rows, LANES), i32),
            pltpu.VMEM((rows, LANES), i32),
            pltpu.VMEM((rows, LANES), revenue.dtype),
            pltpu.VMEM((cands, LANES), i32),
            dma((7,)),
            pltpu.VMEM((Z + 1, 3 * rows, LANES), f32),
            pltpu.VMEM((WIDE, cands * LANES), jnp.bfloat16),
            pltpu.VMEM((R * C * GROUP, WIDE), f32),
            pltpu.VMEM((C, 1, date_words.shape[0]), i32),
            pltpu.VMEM((C, 1, supplier_words.shape[0]), i32),
            pltpu.VMEM((Q - 1, GROUP, WIDE), f32),
            pltpu.VMEM((cands, LANES), f32),
            pltpu.VMEM((Q - 1, cands, LANES), f32),
            pltpu.SemaphoreType.REGULAR((C,)),
            pltpu.SemaphoreType.REGULAR,
            dma((C,)), dma((C,)), dma((C,)), dma((C,)), dma((Z,)), dma((Z + 1,)),
            dma((Q - 1,)), dma((Q - 1,)), dma((Q - 1,)), dma((Q - 1,)),
        ],
        compiler_params=pltpu.CompilerParams(
            collective_id=0, has_side_effects=True, vmem_limit_bytes=KERNEL_VMEM
        ),
        name="revenue",
    )(
        in_hbm(fact_block.reshape(rows, LANES)),
        in_hbm(fact_offset.reshape(rows, LANES)),
        in_hbm(fact_date.reshape(rows, LANES)),
        in_hbm(revenue.reshape(rows, LANES)),
        in_hbm(candidates.reshape(cands, LANES)),
        in_hbm(supplier_words),
        in_hbm(date_words.reshape(1, -1)),
    )
    owned, found, total = pl.pallas_call(
        finish,
        out_shape=(
            jax.ShapeDtypeStruct((SUP_DEV // LANES, LANES), f32),
            jax.ShapeDtypeStruct((cands, LANES), f32),
            jax.ShapeDtypeStruct((1, 1), f32),
        ),
        in_specs=[vmem],
        out_specs=(vmem, vmem, pl.BlockSpec(memory_space=pltpu.SMEM)),
        compiler_params=pltpu.CompilerParams(vmem_limit_bytes=FINISH_VMEM),
        name="finish",
    )(both)
    return owned.reshape(SUP_DEV), found.reshape(candidates.shape), total.reshape(())


def solution(mesh):
    in_specs = (
        P(("row", "col"), None),
        P(("row", "col")),
        P(("row", "col")),
        P(("row", "col")),
        P("col"),
        P("col"),
        P(),
    )
    out_specs = (P(("row", "col")), P(), P())
    body = functools.partial(per_device, mesh.shape["row"], mesh.shape["col"])
    return jax.shard_map(body, mesh=mesh, in_specs=in_specs, out_specs=out_specs, check_vma=False)
```

```python
import functools

import jax
import jax.numpy as jnp
from jax import lax
from jax.experimental import pallas as pl
from jax.experimental.pallas import tpu as pltpu
from jax.sharding import PartitionSpec as P

SUP_DEV = 2048
LANES = 128
WIDE = 2 * LANES
GROUP = SUP_DEV // WIDE
BITS = 30
CORES = 2
SLAB = 4
KERNEL_VMEM = 40 << 20
FINISH_VMEM = 1 << 20
MESH = pl.DeviceIdType.MESH


def div_bits(x):
    return lax.shift_right_logical(x * 2185, 16)


def lookup(row, index):
    table = jnp.broadcast_to(row, index.shape)
    return jnp.take_along_axis(table, index, axis=1, mode="promise_in_bounds")


def kernel(
    rows_axis, cols_axis,
    block_in, offset_in, date_in, rev_in, cand_in, sup_in, dat_in,
    both_ref,
    block_ref, offset_ref, date_ref, rev_ref, cand_ref, load_sem,
    pack, hot, hist, dat_buf, sup_buf, part, cpart, cparts,
    ready, ready_plane, dat_send, dat_recv, sup_send, sup_recv, row_send, row_recv,
    h_send, h_recv, c_send, c_recv,
):
    R, C = rows_axis, cols_axis
    Z, Q = C // CORES, R * CORES
    i, j = lax.axis_index("row"), lax.axis_index("col")
    z, core = j // CORES, j % CORES
    q = i * CORES + core
    n_rows = block_ref.shape[0]
    n_words = sup_in.shape[0]
    per_block = n_words // R
    owned_rows = both_ref.shape[0] - cand_ref.shape[0]
    lines = R * C * GROUP
    tall = min(lines, WIDE)

    pairs = [
        (offset_in, offset_ref), (block_in, block_ref), (date_in, date_ref), (rev_in, rev_ref),
        (cand_in, cand_ref), (dat_in, dat_buf.at[j]), (sup_in, sup_buf.at[j, 0]),
    ]
    loads = [pltpu.make_async_copy(src, dst, load_sem.at[n]) for n, (src, dst) in enumerate(pairs)]
    for load in loads:
        load.start()

    barrier = pltpu.get_barrier_semaphore()

    def loop(low, high, body):
        def step(n, carry):
            body(n)
            return carry

        lax.fori_loop(low, high, step, 0)

    def at_plane(p):
        return (p // CORES, z * CORES + p % CORES)

    def greet(peer):
        pl.semaphore_signal(barrier, inc=1, device_id=peer, device_id_type=MESH)

    loop(j + 1, C, lambda p: greet((i, p)))
    loop(CORES * (i + 1), Q, lambda p: greet(at_plane(p)))

    @pl.when(j + CORES * i > 0)
    def _():
        pl.semaphore_wait(barrier, j + CORES * i)

    def answer(p):
        pl.semaphore_signal(ready.at[j], inc=1, device_id=(i, p), device_id_type=MESH)

    def answer_plane(p):
        pl.semaphore_signal(ready_plane, inc=1, device_id=at_plane(p), device_id_type=MESH)

    def remote(src, dst, send, recv, peer):
        return pltpu.make_async_remote_copy(
            src_ref=src, dst_ref=dst, send_sem=send, recv_sem=recv, device_id=peer, device_id_type=MESH
        )

    def dat_copy(p, source):
        return remote(dat_in, dat_buf.at[source], dat_send.at[p], dat_recv.at[source], (i, p))

    def sup_copy(p, source):
        return remote(sup_in, sup_buf.at[source, 0], sup_send.at[p], sup_recv.at[source], (i, p))

    def row_copy(p, slot):
        return remote(pack.at[z], pack.at[slot], row_send.at[p], row_recv.at[slot], (i, p * CORES + 1 - core))

    loop(0, j, lambda p: dat_copy(p, j).start())
    loop(0, j, answer)
    loop(0, CORES * i, answer_plane)

    for load in loads[:4]:
        load.wait()
    pack[z, :n_rows] = (block_ref[...] * SUP_DEV + offset_ref[...]).astype(jnp.float32)
    pack[z, n_rows : 2 * n_rows] = date_ref[...].astype(jnp.float32)
    pack[z, 2 * n_rows :] = rev_ref[...].astype(jnp.float32)
    loop(0, jnp.minimum(z, 1), lambda p: row_copy(p, z).start())

    for load in loads[4:]:
        load.wait()

    def to_later(p):
        pl.semaphore_wait(ready.at[p], 1)
        dat_copy(p, j).start()

        @pl.when(p % CORES != core)
        def _():
            row_copy(p // CORES, jnp.where(p // CORES == z, Z, z)).start()

    loop(0, j, lambda p: sup_copy(p, j).start())

    cand = cand_ref[...]
    groups = cand.shape[0]
    c_owner = lax.shift_right_logical(cand, 11)
    c_off = cand & (SUP_DEV - 1)
    c_line = c_owner * GROUP + (lax.shift_right_logical(c_off, 7) & (GROUP - 1))
    c_col = lax.shift_right_logical(c_off, 10) * LANES + (c_off & (LANES - 1))
    iota = lax.broadcasted_iota(jnp.int32, (WIDE, LANES), 0)
    for g in range(groups):
        hit = iota == c_col[g : g + 1, :]
        hot[:, g * LANES : (g + 1) * LANES] = jnp.where(hit, 1.0, 0.0).astype(jnp.bfloat16)

    loop(j + 1, C, to_later)
    loop(j + 1, C, lambda p: sup_copy(p, j).start())
    loop(CORES * (z + 1), C, lambda p: dat_copy(p, p).wait_recv())
    loop(1, z, lambda p: row_copy(p, z).start())

    def others(n, me, body):
        loop(0, me, body)
        loop(me + 1, n, body)

    others(CORES * (z + 1), j, lambda p: dat_copy(p, p).wait_recv())
    table = jnp.concatenate(
        [dat_buf[c] for c in range(C)] + [jnp.zeros((1, LANES - C * dat_in.shape[1]), jnp.int32)], axis=1
    )

    short = iota.astype(jnp.int16)
    one, nought = jnp.ones((), jnp.bfloat16), jnp.zeros((), jnp.bfloat16)

    def spread(x, r):
        return jnp.broadcast_to(x[r : r + 1, :], (WIDE, LANES))

    def add_rows(source, base, total, low=0, high=n_rows):
        ids = pack[source, :n_rows].astype(jnp.int32)
        day = pack[source, n_rows : 2 * n_rows].astype(jnp.int32)
        day_word = div_bits(day)
        lit = lax.shift_right_logical(lookup(table, day_word), day - day_word * BITS) & 1
        value = jnp.where(lit == 1, pack[source, 2 * n_rows :], 0.0)
        line = lax.shift_right_logical(ids, 11) * GROUP + (lax.shift_right_logical(ids, 7) & (GROUP - 1)) - base
        column = (lax.shift_right_logical(ids, 10) & 1) * LANES + (ids & (LANES - 1))
        for r in range(low, high, SLAB):
            left = [
                jnp.where(
                    short == spread(line, n).astype(jnp.int16), spread(value, n).astype(jnp.bfloat16), nought
                )[:tall]
                for n in range(r, min(r + SLAB, high))
            ]
            right = [
                jnp.where(short == spread(column, n).astype(jnp.int16), one, nought)
                for n in range(r, min(r + SLAB, high))
            ]
            total = total + lax.dot_general(
                jnp.concatenate(left, axis=1), jnp.concatenate(right, axis=1), (((1,), (1,)), ((), ())),
                preferred_element_type=jnp.float32,
            )
        return total

    def candidates_of(total, base):
        first = total.astype(jnp.bfloat16)
        second = (total - first.astype(jnp.float32)).astype(jnp.bfloat16)
        found = jnp.dot(first, hot[...], preferred_element_type=jnp.float32)
        found = found + jnp.dot(second, hot[...], preferred_element_type=jnp.float32)
        picked = []
        for g in range(groups):
            hit = iota[:tall] == c_line[g : g + 1, :] - base
            picked.append(jnp.sum(jnp.where(hit, found[:, g * LANES : (g + 1) * LANES], 0.0), axis=0, keepdims=True))
        return jnp.concatenate(picked, axis=0)

    empty = jnp.zeros((tall, WIDE), jnp.float32)
    if lines == tall:
        sources = [lax.rem(z + k, Z) for k in range(1, Z)]

        def wait(slots):
            for slot in slots:
                row_copy(z, slot).wait_recv()

        share = n_rows // 2 // SLAB * SLAB

        @pl.when(core == 0)
        def _():
            wait(sources)
            total = add_rows(z, 0, empty, 0, share)
            for slot in sources:
                total = add_rows(slot, 0, total)
            hist[...] = total

        @pl.when(core == 1)
        def _():
            wait([Z] + sources)
            total = add_rows(z, 0, add_rows(Z, 0, empty, share))
            for slot in sources:
                total = add_rows(slot, 0, total)
            hist[...] = total

    else:
        others(Z, z, lambda p: row_copy(p, p).wait_recv())
        loop(0, core, lambda n: row_copy(z, Z).wait_recv())

        def fill(t, carry):
            base = pl.multiple_of(t * tall, tall)

            def add(slot, acc):
                return add_rows(slot, base, acc)

            acc = lax.fori_loop(0, z, add, empty)
            acc = lax.fori_loop(z + 1, Z, add, acc)
            hist[pl.ds(base, tall), :] = lax.fori_loop(0, CORES * core, lambda n, a: add(z + n * (Z - z), a), acc)
            return carry

        lax.fori_loop(0, lines // tall, fill, 0)

    plane = [lax.rem(q + k, Q) for k in range(1, Q)]

    @pl.when(i < R - 1)
    def _():
        pl.semaphore_wait(ready_plane, CORES * (R - 1 - i))

    def lines_of(p):
        owner = (p // CORES) * C + z * CORES + p % CORES
        return hist.at[pl.ds(pl.multiple_of(owner * GROUP, GROUP), GROUP), :]

    h_copies = [
        remote(lines_of(p), part.at[k], h_send.at[k], h_recv.at[k], at_plane(p)) for k, p in enumerate(plane)
    ]
    for copy in h_copies:
        copy.start()

    if lines == tall:
        mine = candidates_of(hist[...], 0)
    else:

        def gather(t, acc):
            base = pl.multiple_of(t * tall, tall)
            return acc + candidates_of(hist[pl.ds(base, tall), :], base)

        mine = lax.fori_loop(0, lines // tall, gather, jnp.zeros(cand.shape, jnp.float32))
    cpart[...] = mine
    c_copies = [
        remote(cpart, cparts.at[k], c_send.at[k], c_recv.at[k], at_plane(p)) for k, p in enumerate(plane)
    ]
    for copy in c_copies:
        copy.start()

    others(C, j, lambda p: sup_copy(p, p).wait_recv())
    full = n_words // LANES

    def words_at(source, flat):
        word = lookup(sup_buf[source, :, n_words - LANES :], jnp.maximum(flat - (n_words - LANES), 0))
        for t in range(full):
            near = (flat >= t * LANES) & (flat < (t + 1) * LANES)
            word = jnp.where(near, lookup(sup_buf[source, :, t * LANES : (t + 1) * LANES], flat & (LANES - 1)), word)
        return word

    c_word = div_bits(c_off)
    c_bit = c_off - c_word * BITS
    c_source = lax.div(c_owner, R)
    c_flat = (c_owner - c_source * R) * per_block + c_word

    def word_of(source, acc):
        return jnp.where(c_source == source, words_at(source, c_flat), acc)

    c_words = lax.fori_loop(0, C, word_of, jnp.zeros(cand.shape, jnp.int32))
    c_lit = (lax.shift_right_logical(c_words, c_bit) & 1) == 1

    me = i * C + j
    shape = (owned_rows, LANES)
    spot = lax.broadcasted_iota(jnp.int32, shape, 0) * LANES + lax.broadcasted_iota(jnp.int32, shape, 1)
    spot_word = div_bits(spot)
    my_words = words_at(me // R, lax.rem(me, R) * per_block + spot_word)
    my_lit = (lax.shift_right_logical(my_words, spot - spot_word * BITS) & 1) == 1

    owned = hist[pl.ds(pl.multiple_of(me * GROUP, GROUP), GROUP), :]
    for k, copy in enumerate(h_copies):
        copy.wait_recv()
        owned = owned + part[k]
    both_ref[:GROUP, :] = jnp.where(my_lit[:GROUP], owned[:, :LANES], 0.0)
    both_ref[GROUP:owned_rows, :] = jnp.where(my_lit[GROUP:], owned[:, LANES:], 0.0)

    found = cpart[...]
    for k, copy in enumerate(c_copies):
        copy.wait_recv()
        found = found + cparts[k]
    both_ref[owned_rows:, :] = jnp.where(c_lit, found, 0.0)

    others(C, j, lambda p: dat_copy(p, j).wait_send())
    others(C, j, lambda p: sup_copy(p, j).wait_send())
    others(Z, z, lambda p: row_copy(p, z).wait_send())
    loop(core, 1, lambda n: row_copy(z, Z).wait_send())
    for copy in h_copies + c_copies:
        copy.wait_send()


def in_hbm(x):
    return pltpu.with_memory_space_constraint(x, pltpu.HBM)


def finish(both_ref, owned_ref, cand_out_ref, total_ref):
    owned_rows = owned_ref.shape[0]
    owned_ref[...] = both_ref[:owned_rows, :]
    found = both_ref[owned_rows:, :]
    cand_out_ref[...] = found
    total_ref[0, 0] = jnp.sum(found)


def per_device(R, C, fact_block, fact_offset, fact_date, revenue, supplier_words, date_words, candidates):
    rows = fact_offset.shape[0] // LANES
    cands = candidates.shape[0] // LANES
    Z, Q = C // CORES, R * CORES
    f32, i32 = jnp.float32, jnp.int32
    dma = pltpu.SemaphoreType.DMA
    vmem = pl.BlockSpec(memory_space=pltpu.VMEM)
    both = pl.pallas_call(
        functools.partial(kernel, R, C),
        out_shape=jax.ShapeDtypeStruct((SUP_DEV // LANES + cands, LANES), f32),
        in_specs=[pl.BlockSpec(memory_space=pl.ANY)] * 7,
        out_specs=vmem,
        scratch_shapes=[
            pltpu.VMEM((rows, LANES), i32),
            pltpu.VMEM((rows, LANES), i32),
            pltpu.VMEM((rows, LANES), i32),
            pltpu.VMEM((rows, LANES), revenue.dtype),
            pltpu.VMEM((cands, LANES), i32),
            dma((7,)),
            pltpu.VMEM((Z + 1, 3 * rows, LANES), f32),
            pltpu.VMEM((WIDE, cands * LANES), jnp.bfloat16),
            pltpu.VMEM((R * C * GROUP, WIDE), f32),
            pltpu.VMEM((C, 1, date_words.shape[0]), i32),
            pltpu.VMEM((C, 1, supplier_words.shape[0]), i32),
            pltpu.VMEM((Q - 1, GROUP, WIDE), f32),
            pltpu.VMEM((cands, LANES), f32),
            pltpu.VMEM((Q - 1, cands, LANES), f32),
            pltpu.SemaphoreType.REGULAR((C,)),
            pltpu.SemaphoreType.REGULAR,
            dma((C,)), dma((C,)), dma((C,)), dma((C,)), dma((Z,)), dma((Z + 1,)),
            dma((Q - 1,)), dma((Q - 1,)), dma((Q - 1,)), dma((Q - 1,)),
        ],
        compiler_params=pltpu.CompilerParams(
            collective_id=0, has_side_effects=True, vmem_limit_bytes=KERNEL_VMEM
        ),
        name="revenue",
    )(
        in_hbm(fact_block.reshape(rows, LANES)),
        in_hbm(fact_offset.reshape(rows, LANES)),
        in_hbm(fact_date.reshape(rows, LANES)),
        in_hbm(revenue.reshape(rows, LANES)),
        in_hbm(candidates.reshape(cands, LANES)),
        in_hbm(supplier_words),
        in_hbm(date_words.reshape(1, -1)),
    )
    owned, found, total = pl.pallas_call(
        finish,
        out_shape=(
            jax.ShapeDtypeStruct((SUP_DEV // LANES, LANES), f32),
            jax.ShapeDtypeStruct((cands, LANES), f32),
            jax.ShapeDtypeStruct((1, 1), f32),
        ),
        in_specs=[vmem],
        out_specs=(vmem, vmem, pl.BlockSpec(memory_space=pltpu.SMEM)),
        compiler_params=pltpu.CompilerParams(vmem_limit_bytes=FINISH_VMEM),
        name="finish",
    )(both)
    return owned.reshape(SUP_DEV), found.reshape(candidates.shape), total.reshape(())


def solution(mesh):
    in_specs = (
        P(("row", "col"), None),
        P(("row", "col")),
        P(("row", "col")),
        P(("row", "col")),
        P("col"),
        P("col"),
        P(),
    )
    out_specs = (P(("row", "col")), P(), P())
    body = functools.partial(per_device, mesh.shape["row"], mesh.shape["col"])
    return jax.shard_map(body, mesh=mesh, in_specs=in_specs, out_specs=out_specs, check_vma=False)
```
